32 devices in a mesh: group: 4 (over z), patch: 8 (over y, x, core).
Axes of the slice: x: 2, y: 2, z: 4, core: 2. Of those that a mesh axis runs over, the one named last changes fastest.
Arguments:
- volume: float32 [4096, 8, 1024], P(('group', 'patch')), may hold values from 0.02 to 18, as said below
- block_place: int32 [4096], P(('group', 'patch')), may hold values from 0 to 4095, as said below
- measured: float32 [2, 512, 384], P(None, 'patch'), may hold values from 0.5 to 5.5
- live_rays: int32 [2, 512], replicated, may hold values from 24 to 48
Outputs:
- final_volume: float32 [4096, 8, 1024], P(('group', 'patch'))
- last_residual: float32 [4, 128, 384], P('group', 'patch')
The draws below stay inside these ranges and needn't reach their ends.
Inputs may be any that keep to these rules, and one draw needn't show every extreme that they name: block_place lists the block positions of the 64 x 64 grid in the order of a Hilbert curve over that grid, begun at a drawn point of the curve (continuing from its end to its start) and turned or mirrored by one of the grid's eight symmetries; each position appears once. `volume`: positive.
All inputs are finite; a program needn't handle non-finite values.
Results may differ from the reference program's by a relative error of at most 0.0007.
Values may be sent and summed in bfloat16 or wider, within the bound.
A program may use at most 192 MiB of HBM per device.

```python
import math
import jax
import jax.numpy as jnp
from jax import lax

NSL = 8
IMG_BLK = 64
BLK_SIDE = 32
RAYS_TILE = 48
NTILE = 64
ANG_SUB = 8
SUBSETS = 2
NBLK = 4096
ROWS = 512
N_GROUP = 4
N_PATCH = 8


def draw_volume(key, part):
    scale_key, texture_key = jax.random.split(jax.random.fold_in(key, 17))
    brightness = jnp.exp(jax.random.uniform(scale_key, (NBLK, 1, 1), jnp.float32, -2.3, 2.3))
    texture = jax.random.uniform(texture_key, (NBLK, NSL, BLK_SIDE * BLK_SIDE), jnp.float32, 0.5, 1.5)
    return brightness * texture


def draw_block_place(key, part):
    symmetry_key, start_key = jax.random.split(jax.random.fold_in(key, 29))
    symmetry = jax.random.randint(symmetry_key, (3,), 0, 2, jnp.int32)
    start = jax.random.randint(start_key, (), 0, NBLK, jnp.int32)
    walk = (jnp.arange(NBLK, dtype=jnp.int32) + start) % NBLK
    column = jnp.zeros((NBLK,), jnp.int32)
    row_pos = jnp.zeros((NBLK,), jnp.int32)
    level = 1
    while level < IMG_BLK:
        right_bit = walk // 2 % 2
        upper_bit = (walk + right_bit) % 2
        upper_bit = jnp.where(right_bit == 1, 1 - walk % 2, walk % 2)
        flipped = (upper_bit == 0) & (right_bit == 1)
        column = jnp.where(flipped, level - 1 - column, column)
        row_pos = jnp.where(flipped, level - 1 - row_pos, row_pos)
        turned = upper_bit == 0
        column, row_pos = (jnp.where(turned, row_pos, column), jnp.where(turned, column, row_pos))
        column = column + level * right_bit
        row_pos = row_pos + level * upper_bit
        walk = walk // 4
        level = level * 2
    column = jnp.where(symmetry[0] == 1, IMG_BLK - 1 - column, column)
    row_pos = jnp.where(symmetry[1] == 1, IMG_BLK - 1 - row_pos, row_pos)
    column, row_pos = (jnp.where(symmetry[2] == 1, row_pos, column), jnp.where(symmetry[2] == 1, column, row_pos))
    return (row_pos * IMG_BLK + column).astype(jnp.int32)


def with_ends(values, key, smallest, largest):
    spot = [jax.random.randint(jax.random.fold_in(key, axis), (), 0, length) for axis, length in enumerate(values.shape)]
    longest = values.shape.index(max(values.shape))
    neighbour = spot[:longest] + [(spot[longest] + 1) % values.shape[longest]] + spot[longest + 1:]
    return values.at[tuple(spot)].set(smallest).at[tuple(neighbour)].set(largest)


def levels(stream_key, dims, shards, low, top_value):
    def one(position, parts):
        steps = jax.random.uniform(jax.random.fold_in(jax.random.fold_in(stream_key, 6), position), (parts,), jnp.float32, low / len(shards), top_value / len(shards))
        return jnp.repeat(jnp.exp(steps), dims[position] // parts).reshape((-1,) + (1,) * (len(dims) - position - 1))

    factor_of = one(*shards[0])
    for cut in shards[1:]:
        factor_of = factor_of * one(*cut)
    return factor_of


def setup_inputs(seed: int = 0) -> dict:
    splits = jax.random.split(jax.random.key(seed), 5)
    volume = draw_volume(jax.random.fold_in(splits[4], 71), 0)
    block_place = draw_block_place(jax.random.fold_in(splits[4], 71), 0)
    measured = jnp.clip(0.5 + 5.0 * jax.random.uniform(splits[2], (SUBSETS, ROWS, RAYS_TILE * NSL), jnp.float32) ** levels(splits[2], (SUBSETS, ROWS, RAYS_TILE * NSL), ((1, 8),), -0.2, 0.2), 0.5, 5.5)
    live_rays = with_ends(jax.random.randint(splits[3], (SUBSETS, ROWS), 24, 49), jax.random.fold_in(splits[3], 1), 24, 48).astype(jnp.int32)
    return {"volume": volume, "block_place": block_place, "measured": measured, "live_rays": live_rays}


spread = 1.5
relax = 0.9


def footprint_tiles(place, angle_value):
    cosine = jnp.cos(angle_value)
    sine_value = jnp.sin(angle_value)
    half_image = IMG_BLK * BLK_SIDE * 0.5
    half_detector = NTILE * RAYS_TILE * 0.5
    block_col = (place % IMG_BLK).astype(jnp.float32) * BLK_SIDE - half_image
    block_row = (place // IMG_BLK).astype(jnp.float32) * BLK_SIDE - half_image
    centre = (block_col + BLK_SIDE * 0.5) * cosine + (block_row + BLK_SIDE * 0.5) * sine_value
    first_tile = jnp.floor((centre + half_detector - RAYS_TILE * 0.5) / RAYS_TILE).astype(jnp.int32)
    voxel = jnp.arange(BLK_SIDE * BLK_SIDE, dtype=jnp.int32)
    offset_col = (voxel % BLK_SIDE).astype(jnp.float32) + 0.5
    offset_row = (voxel // BLK_SIDE).astype(jnp.float32) + 0.5
    along = (block_col[:, None] + offset_col[None, :]) * cosine + (block_row[:, None] + offset_row[None, :]) * sine_value
    ray_ids = first_tile[:, None] * RAYS_TILE + jnp.arange(2 * RAYS_TILE, dtype=jnp.int32)[None, :]
    detector = ray_ids.astype(jnp.float32) + 0.5 - half_detector
    scaled = (along[:, None, :] - detector[:, :, None]) / spread
    bump = jnp.maximum(1.0 - scaled * scaled, 0.0)
    return first_tile, (bump * bump).astype(jnp.bfloat16)


def angle_of(angle, subset):
    return jnp.asarray(math.pi * (angle * SUBSETS + subset) / (ANG_SUB * SUBSETS), jnp.float32)


def tile_rows(angle, first_tile):
    return (angle * NTILE + first_tile[:, None] + jnp.arange(2, dtype=jnp.int32)[None, :]).reshape(-1)


def forward(rounded, place, subset):
    blocks, slices = rounded.shape[0], rounded.shape[1]
    projection = jnp.zeros((ANG_SUB * NTILE, RAYS_TILE * slices), jnp.float32)
    ray_sum = jnp.zeros((ANG_SUB * NTILE, RAYS_TILE), jnp.float32)
    col_sum = jnp.zeros((blocks, BLK_SIDE * BLK_SIDE), jnp.float32)
    for angle in range(ANG_SUB):
        first_tile, footprint = footprint_tiles(place, angle_of(angle, subset))
        row_ids = tile_rows(angle, first_tile)
        contrib = jnp.einsum("brv,bsv->brs", footprint.astype(jnp.float32), rounded.astype(jnp.float32))
        projection = projection.at[row_ids].add(contrib.reshape(2 * blocks, RAYS_TILE * slices))
        ray_part = jnp.sum(footprint.astype(jnp.float32), axis=2)
        ray_sum = ray_sum.at[row_ids].add(ray_part.reshape(2 * blocks, RAYS_TILE))
        col_sum = col_sum + jnp.sum(footprint.astype(jnp.float32), axis=1)
    return projection, ray_sum, col_sum


def backward(residual_b, place, subset):
    blocks = place.shape[0]
    slices = residual_b.shape[1] // RAYS_TILE
    total = jnp.zeros((blocks, slices, BLK_SIDE * BLK_SIDE), jnp.float32)
    for angle in range(ANG_SUB):
        first_tile, footprint = footprint_tiles(place, angle_of(angle, subset))
        picked = residual_b[tile_rows(angle, first_tile)].reshape(blocks, 2 * RAYS_TILE, slices)
        total = total + jnp.einsum("brv,brs->bsv", footprint.astype(jnp.float32), picked.astype(jnp.float32))
    return total


def residual_of(projection, ray_sum, measured_rows, live_count):
    count = projection.shape[0]
    live = (jnp.arange(RAYS_TILE, dtype=jnp.int32)[None, :] < live_count[:, None]).astype(jnp.float32)
    level = projection.reshape(count, RAYS_TILE, -1) / jnp.maximum(ray_sum, 1.0)[:, :, None]
    differ = (measured_rows.reshape(count, RAYS_TILE, -1) - level) * live[:, :, None]
    return differ.reshape(count, -1)


def reference(volume, block_place, measured, live_rays):
    estimate = volume
    slices = volume.shape[1]
    width = RAYS_TILE * slices
    batches = NBLK // 64
    place_groups = block_place.reshape(batches, 64)
    residual = jnp.zeros((ANG_SUB * NTILE, width), jnp.float32)
    for subset in range(SUBSETS):
        rounded = estimate.astype(jnp.bfloat16).reshape(batches, 64, slices, BLK_SIDE * BLK_SIDE)

        def forward_step(totals, member):
            projection, ray_sum, col_sum = forward(member[0], member[1], subset)
            return (totals[0] + projection, totals[1] + ray_sum), col_sum

        start = (jnp.zeros((ANG_SUB * NTILE, width), jnp.float32), jnp.zeros((ANG_SUB * NTILE, RAYS_TILE), jnp.float32))
        totals, col_sums = lax.scan(forward_step, start, (rounded, place_groups))
        col_sum = col_sums.reshape(NBLK, BLK_SIDE * BLK_SIDE)
        residual = residual_of(totals[0], totals[1], measured[subset], live_rays[subset])
        residual_b = residual.astype(jnp.bfloat16)
        backprojected = lax.map(lambda place: backward(residual_b, place, subset), place_groups)
        backprojected = backprojected.reshape(NBLK, slices, BLK_SIDE * BLK_SIDE)
        estimate = jnp.maximum(estimate + relax * backprojected / col_sum[:, None, :], 0.0)
    share_rows = ANG_SUB * NTILE // (N_GROUP * N_PATCH)
    last_residual = residual.reshape(N_PATCH, N_GROUP, share_rows, width).transpose(1, 0, 2, 3)
    return estimate, last_residual.reshape(N_GROUP, N_PATCH * share_rows, width)
```

```python
import math

import jax
import jax.numpy as jnp
import numpy as np
from jax import lax
from jax.experimental import pallas as pl
from jax.experimental.pallas import tpu as pltpu
from jax.sharding import PartitionSpec as P

IMG_BLK = 64
BLK_SIDE = 32
RAYS_TILE = 48
NTILE = 64
ANG_SUB = 8
SUBSETS = 2

spread = 1.5
relax = 0.9

SUB = 8
NQ = (BLK_SIDE // SUB) ** 2
R = 16
VOX = BLK_SIDE * BLK_SIDE
RAYS = NTILE * RAYS_TILE
LANES = 128
PAD = 32
TALL = RAYS + 2 * PAD
SPAN = 128
VMEM_LIMIT = 60 * 1024 * 1024


def angles(subset):
    return [math.pi * (a * SUBSETS + subset) / (ANG_SUB * SUBSETS) for a in range(ANG_SUB)]


def geometry(subset):
    v = np.arange(VOX)
    col = (v % BLK_SIDE) + 0.5 - BLK_SIDE / 2
    row = (v // BLK_SIDE) + 0.5 - BLK_SIDE / 2
    q_of = (v // BLK_SIDE // SUB) * (BLK_SIDE // SUB) + (v % BLK_SIDE) // SUB
    base = np.zeros((ANG_SUB, VOX), np.float64)
    first = np.zeros((ANG_SUB, NQ), np.int64)
    for a, theta in enumerate(angles(subset)):
        off = col * math.cos(theta) + row * math.sin(theta)
        for q in range(NQ):
            mine = q_of == q
            first[a, q] = math.floor(off[mine].min() - spread)
            base[a, mine] = off[mine] - first[a, q]
    return base.astype(np.float32), first.astype(np.int32)


def fill_grid(base_ref, e_scr):
    ray = lax.broadcasted_iota(jnp.int32, (R, VOX), 0).astype(jnp.float32)
    for a in range(ANG_SUB):
        e_scr[a * R:(a + 1) * R, :] = (base_ref[a:a + 1, :] - ray) * (1.0 / spread)


def make_footprint(e_scr, f_scr, frac_ref, b):
    for a in range(ANG_SUB):
        t = e_scr[a * R:(a + 1) * R, :] + frac_ref[b, a]
        bump = jnp.maximum(1.0 - t * t, 0.0)
        f_scr[a * R:(a + 1) * R, :] = (bump * bump).astype(jnp.bfloat16)


def merge_range(win_ref, a):
    begin = jnp.maximum(win_ref[0, a] - PAD, 0) // SPAN
    end = jnp.minimum((win_ref[1, a] + R + PAD) // SPAN + 1, RAYS // SPAN)
    return begin, end


def aligned(x, m):
    return pl.multiple_of(x, m)


def forward_kernel(nb, lo_ref, frac_ref, win_ref, first_ref, vol_ref, base_ref, out_ref,
                   e_scr, f_scr, m_scr, acc):
    step = pl.program_id(0)

    @pl.when(step == 0)
    def _():
        fill_grid(base_ref, e_scr)
        v = lax.broadcasted_iota(jnp.int32, (LANES, VOX), 1)
        line = lax.broadcasted_iota(jnp.int32, (LANES, VOX), 0)
        q_of = (v // (BLK_SIDE * SUB)) * (BLK_SIDE // SUB) + (v % BLK_SIDE) // SUB
        m_scr[...] = jnp.where(q_of == line // 8, 1.0, 0.0).astype(jnp.bfloat16)
        zero = jnp.zeros((64, LANES), jnp.float32)

        def clear_angle(a, c):
            begin, end = merge_range(win_ref, a)
            begin = begin * (SPAN // 64)
            end = end * (SPAN // 64) + 1

            def clear(i, c):
                acc[pl.ds(aligned(a * TALL + i * 64, 64), 64), :] = zero
                return c

            return lax.fori_loop(begin, end, clear, c)

        lax.fori_loop(0, ANG_SUB, clear_angle, 0)

    def one(i, c):
        b = step * nb + i
        make_footprint(e_scr, f_scr, frac_ref, b)
        rounded = vol_ref[i].astype(jnp.bfloat16)
        spreadv = jnp.tile(rounded, (NQ, 1)) * m_scr[...]
        part = lax.dot_general(f_scr[...], spreadv, (((1,), (1,)), ((), ())),
                               preferred_element_type=jnp.float32)
        for a in range(ANG_SUB):
            at = pl.ds(a * TALL + PAD + lo_ref[b, a], R)
            acc[at, :] += part[a * R:(a + 1) * R, :]
        return c

    lax.fori_loop(0, nb, one, 0, unroll=2)

    @pl.when(step == pl.num_programs(0) - 1)
    def _():
        out_ref[...] = jnp.zeros_like(out_ref)
        span = SPAN
        lane_q = lax.broadcasted_iota(jnp.int32, (span, LANES), 1) // 8
        row_j = lax.broadcasted_iota(jnp.int32, (span, LANES), 0) % 16
        pick = lane_q == row_j

        def merge_angle(a, c):
            begin, end = merge_range(win_ref, a)

            def merge(i, c):
                k = i * span
                total = jnp.zeros((span, LANES), jnp.float32)
                for q in range(NQ):
                    src = a * TALL + PAD + k - first_ref[a, q]
                    total = jnp.where(lane_q == q, acc[pl.ds(src, span), :], total)
                for s in (64, 32, 16, 8):
                    total = total + pltpu.roll(total, s, 1)
                total = jnp.where(pick, total, 0.0)
                out = jnp.sum(total.reshape(span // 16, 16, LANES), axis=1)
                out_ref[pl.ds(aligned(a * (RAYS // 16) + i * 8, 8), 8), :] = out
                return c

            return lax.fori_loop(begin, end, merge, c)

        lax.fori_loop(0, ANG_SUB, merge_angle, 0)


def backward_kernel(nb, lo_ref, frac_ref, win_ref, first_ref, vol_ref, base_ref, res_ref, out_ref,
                    e_scr, f_scr, rb, dd):
    step = pl.program_id(0)

    @pl.when(step == 0)
    def _():
        fill_grid(base_ref, e_scr)
        span = SPAN
        lane_q = lax.broadcasted_iota(jnp.int32, (span, LANES), 1) // 8
        row_j = lax.broadcasted_iota(jnp.int32, (span, LANES), 0) % 16
        pick = lane_q == row_j
        fold = jnp.where(
            lax.broadcasted_iota(jnp.int32, (LANES, LANES), 0) % 8
            == lax.broadcasted_iota(jnp.int32, (LANES, LANES), 1) % 8, 1.0, 0.0).astype(jnp.bfloat16)

        def one_angle(a, c):
            begin = jnp.maximum((win_ref[0, a] - 64) // span, 0)
            end = jnp.minimum((win_ref[1, a] + 64 + span) // span + 1, RAYS // span)

            def widen(i, c):
                rows = res_ref[pl.ds(aligned(a * (RAYS // 16) + i * 8, 8), 8), :]
                wide = jnp.broadcast_to(rows[:, None, :], (8, 16, LANES)).reshape(span, LANES)
                wide = jnp.where(pick, wide, 0.0).astype(jnp.bfloat16)
                rb[pl.ds(aligned(PAD + i * span, 8), span), :] = jnp.dot(
                    wide, fold, preferred_element_type=jnp.float32)
                return c

            lax.fori_loop(begin, end, widen, 0)
            first = jnp.maximum(win_ref[0, a] // span, 0)
            last = jnp.minimum((win_ref[1, a] + 16) // span + 1, RAYS // span)

            def shift(i, c):
                k = i * span
                total = jnp.zeros((span, LANES), jnp.float32)
                for q in range(NQ):
                    src = PAD + k + first_ref[a, q]
                    total = jnp.where(lane_q == q, rb[pl.ds(src, span), :], total)
                dd[pl.ds(aligned(a * RAYS + k, span), span), :] = total
                return c

            lax.fori_loop(first, last, shift, 0)
            return c

        lax.fori_loop(0, ANG_SUB, one_angle, 0)

    width = SUB * BLK_SIDE
    group = BLK_SIDE // SUB
    lane = lax.broadcasted_iota(jnp.int32, (8, width), 1)
    col_group = (lane % BLK_SIDE) // SUB

    def one(i, c):
        b = step * nb + i
        make_footprint(e_scr, f_scr, frac_ref, b)
        rows = jnp.concatenate(
            [dd[pl.ds(a * RAYS + lo_ref[b, a], R), :] for a in range(ANG_SUB)], axis=0)
        turned = jnp.transpose(rows)
        ones = jnp.ones((8, ANG_SUB * R), jnp.float32)
        for g in range(group):
            lhs = jnp.concatenate([turned[g * 32:(g + 1) * 32], ones], axis=0).astype(jnp.bfloat16)
            at = slice(g * width, (g + 1) * width)
            part = jnp.dot(lhs, f_scr[:, at], preferred_element_type=jnp.float32)
            back = part[0:8]
            for j in range(1, group):
                back = jnp.where(col_group == j, part[j * 8:(j + 1) * 8], back)
            col_sum = part[32:40]
            out_ref[i, :, at] = jnp.maximum(vol_ref[i, :, at] + relax * back / col_sum, 0.0)
        return c

    lax.fori_loop(0, nb, one, 0, unroll=2)


def ray_sum_kernel(c_ref, s_ref, k_ref, out_ref):
    side = IMG_BLK * BLK_SIDE
    half = side * 0.5
    for u in range(c_ref.shape[0]):
        cs = c_ref[u] * (1.0 / spread)
        sn = s_ref[u] * (1.0 / spread)
        inv = 1.0 / cs
        ray = k_ref[u] * (1.0 / spread)

        def row(i, total):
            y = i.astype(jnp.float32) + (0.5 - half)
            w = ray - y * sn
            mid = jnp.floor(w * inv) + 0.5
            t0 = mid * cs - w
            for j in range(-2, 3):
                t = t0 + j * cs
                bump = jnp.maximum(1.0 - t * t, 0.0)
                total = total + jnp.where(jnp.abs(mid + j) < half, bump * bump, 0.0)
            return total

        out_ref[u] = lax.fori_loop(0, side, row, jnp.zeros(out_ref.shape[1:], jnp.float32), unroll=8)


def smem():
    return pl.BlockSpec(memory_space=pltpu.SMEM)


def forward(volume, lo, frac, win, base, first):
    blocks, slices, _ = volume.shape
    nb = 8
    lines = ANG_SUB * RAYS // 16
    return pl.pallas_call(
        lambda *refs: forward_kernel(nb, *refs),
        grid=(blocks // nb,),
        in_specs=[smem(), smem(), smem(), smem(),
                  pl.BlockSpec((nb, slices, VOX), lambda i: (i, 0, 0)),
                  pl.BlockSpec((ANG_SUB, VOX), lambda i: (0, 0))],
        out_specs=pl.BlockSpec((lines, LANES), lambda i: (0, 0)),
        out_shape=jax.ShapeDtypeStruct((lines, LANES), jnp.float32),
        scratch_shapes=[pltpu.VMEM((ANG_SUB * R, VOX), jnp.float32),
                        pltpu.VMEM((ANG_SUB * R, VOX), jnp.bfloat16),
                        pltpu.VMEM((LANES, VOX), jnp.bfloat16),
                        pltpu.VMEM((ANG_SUB * TALL, LANES), jnp.float32)],
        compiler_params=pltpu.CompilerParams(vmem_limit_bytes=VMEM_LIMIT),
        name="forward",
    )(lo, frac, win, first, volume, base)


def backward(volume, residual, lo, frac, win, base, first):
    blocks, slices, _ = volume.shape
    nb = 8
    return pl.pallas_call(
        lambda *refs: backward_kernel(nb, *refs),
        grid=(blocks // nb,),
        in_specs=[smem(), smem(), smem(), smem(),
                  pl.BlockSpec((nb, slices, VOX), lambda i: (i, 0, 0)),
                  pl.BlockSpec((ANG_SUB, VOX), lambda i: (0, 0)),
                  pl.BlockSpec(residual.shape, lambda i: (0, 0))],
        out_specs=pl.BlockSpec((nb, slices, VOX), lambda i: (i, 0, 0)),
        out_shape=jax.ShapeDtypeStruct(volume.shape, jnp.float32),
        scratch_shapes=[pltpu.VMEM((ANG_SUB * R, VOX), jnp.float32),
                        pltpu.VMEM((ANG_SUB * R, VOX), jnp.bfloat16),
                        pltpu.VMEM((TALL, LANES), jnp.float32),
                        pltpu.VMEM((ANG_SUB * RAYS, LANES), jnp.float32)],
        compiler_params=pltpu.CompilerParams(vmem_limit_bytes=VMEM_LIMIT),
        name="backward",
    )(lo, frac, win, first, volume, base, residual)


def own_ray_sums(first_row, rows):
    count = rows * RAYS_TILE
    padded = -(-count // 1024) * 1024
    idx = jnp.minimum(jnp.arange(padded, dtype=jnp.int32), count - 1)
    row = first_row + idx // RAYS_TILE
    ray = ((row % NTILE) * RAYS_TILE + idx % RAYS_TILE).astype(jnp.float32) + (0.5 - RAYS * 0.5)
    angle = row // NTILE
    big, small = [], []
    for subset in range(SUBSETS):
        th = angles(subset)
        pairs = [sorted((math.cos(t), math.sin(t)), key=abs) for t in th]
        sign = jnp.zeros((padded,), jnp.float32)
        b, s = sign, sign
        for a in range(ANG_SUB):
            b = jnp.where(angle == a, np.float32(pairs[a][1]), b)
            s = jnp.where(angle == a, np.float32(pairs[a][0]), s)
        big.append(b)
        small.append(s)
    shape = (SUBSETS, padded // LANES, LANES)
    big = jnp.stack(big).reshape(shape)
    small = jnp.stack(small).reshape(shape)
    rays = jnp.broadcast_to(ray.reshape(1, padded // LANES, LANES), shape)
    sums = pl.pallas_call(
        ray_sum_kernel,
        out_shape=jax.ShapeDtypeStruct(shape, jnp.float32),
        name="raysum",
    )(big, small, rays)
    return sums.reshape(SUBSETS, padded)[:, :count]


def placing(place, subset):
    half = IMG_BLK * BLK_SIDE * 0.5
    x = (place % IMG_BLK).astype(jnp.float32) * BLK_SIDE + (BLK_SIDE * 0.5 - half)
    y = (place // IMG_BLK).astype(jnp.float32) * BLK_SIDE + (BLK_SIDE * 0.5 - half)
    cosine = np.cos(np.array(angles(subset))).astype(np.float32)
    sine = np.sin(np.array(angles(subset))).astype(np.float32)
    z = x[:, None] * cosine + y[:, None] * sine + (RAYS * 0.5 - 0.5)
    low = jnp.floor(z)
    lo = low.astype(jnp.int32)
    win = jnp.stack([jnp.min(lo, axis=0), jnp.max(lo, axis=0)])
    return lo, (z - low) * (1.0 / spread), win


def shards(volume, block_place, measured, live_rays):
    groups = lax.axis_size("group")
    patches = lax.axis_size("patch")
    group_index = lax.axis_index("group")
    patch_index = lax.axis_index("patch")
    slices = volume.shape[1]
    slab_rows = ANG_SUB * NTILE // patches
    rows = slab_rows // groups
    first_row = patch_index * slab_rows + group_index * rows
    lines = rows * RAYS_TILE * slices // LANES
    per = LANES // slices
    sums = own_ray_sums(first_row, rows)
    estimate = volume
    own_residual = None
    for subset in range(SUBSETS):
        base, first = geometry(subset)
        lo, frac, win = placing(block_place, subset)
        partial = forward(estimate, lo, frac, win, base, first)
        total = lax.psum_scatter(partial, ("patch", "group"), scatter_dimension=0, tiled=True)
        mine = lax.dynamic_slice_in_dim(measured[subset], group_index * rows, rows, 0)
        live = lax.dynamic_slice_in_dim(live_rays[subset], first_row, rows, 0)
        on = jnp.arange(RAYS_TILE, dtype=jnp.int32)[None, :] < live[:, None]
        on = jnp.broadcast_to(on[:, :, None], (rows, RAYS_TILE, slices)).reshape(lines, LANES)
        rs = jnp.maximum(sums[subset], 1.0).reshape(lines, per, 1)
        rs = jnp.broadcast_to(rs, (lines, per, slices)).reshape(lines, LANES)
        residual = jnp.where(on, mine.reshape(lines, LANES) - total / rs, 0.0)
        own_residual = residual.reshape(rows, RAYS_TILE * slices)
        full = lax.all_gather(residual.astype(jnp.bfloat16), ("patch", "group"), axis=0, tiled=True)
        estimate = backward(estimate, full.astype(jnp.float32), lo, frac, win, base, first)
    return (estimate, own_residual[None])


def solution(mesh):
    return jax.shard_map(
        shards,
        mesh=mesh,
        in_specs=(
            P(("group", "patch"), None, None),
            P(("group", "patch")),
            P(None, "patch", None),
            P(),
        ),
        out_specs=(P(("group", "patch"), None, None), P("group", "patch", None)),
        check_vma=False,
    )
```

```python
import math

import jax
import jax.numpy as jnp
import numpy as np
from jax import lax
from jax.experimental import pallas as pl
from jax.experimental.pallas import tpu as pltpu
from jax.sharding import PartitionSpec as P

IMG_BLK = 64
BLK_SIDE = 32
RAYS_TILE = 48
NTILE = 64
ANG_SUB = 8
SUBSETS = 2

spread = 1.5
relax = 0.9

SUB = 8
NQ = (BLK_SIDE // SUB) ** 2
R = 16
VOX = BLK_SIDE * BLK_SIDE
RAYS = NTILE * RAYS_TILE
LANES = 128
PAD = 32
TALL = RAYS + 2 * PAD
SPAN = 128
VMEM_LIMIT = 60 * 1024 * 1024


def angles(subset):
    return [math.pi * (a * SUBSETS + subset) / (ANG_SUB * SUBSETS) for a in range(ANG_SUB)]


def geometry(subset):
    v = np.arange(VOX)
    col = (v % BLK_SIDE) + 0.5 - BLK_SIDE / 2
    row = (v // BLK_SIDE) + 0.5 - BLK_SIDE / 2
    q_of = (v // BLK_SIDE // SUB) * (BLK_SIDE // SUB) + (v % BLK_SIDE) // SUB
    base = np.zeros((ANG_SUB, VOX), np.float64)
    first = np.zeros((ANG_SUB, NQ), np.int64)
    for a, theta in enumerate(angles(subset)):
        off = col * math.cos(theta) + row * math.sin(theta)
        for q in range(NQ):
            mine = q_of == q
            first[a, q] = math.floor(off[mine].min() - spread)
            base[a, mine] = off[mine] - first[a, q]
    return base.astype(np.float32), first.astype(np.int32)


def fill_grid(base_ref, e_scr):
    ray = lax.broadcasted_iota(jnp.int32, (R, VOX), 0).astype(jnp.float32)
    for a in range(ANG_SUB):
        e_scr[a * R:(a + 1) * R, :] = (base_ref[a:a + 1, :] - ray) * (1.0 / spread)


def make_footprint(e_scr, f_scr, frac_ref, b):
    for a in range(ANG_SUB):
        t = e_scr[a * R:(a + 1) * R, :] + frac_ref[b, a]
        bump = jnp.maximum(1.0 - t * t, 0.0)
        f_scr[a * R:(a + 1) * R, :] = (bump * bump).astype(jnp.bfloat16)


def merge_range(win_ref, a):
    begin = jnp.maximum(win_ref[0, a] - PAD, 0) // SPAN
    end = jnp.minimum((win_ref[1, a] + R + PAD) // SPAN + 1, RAYS // SPAN)
    return begin, end


def aligned(x, m):
    return pl.multiple_of(x, m)


def forward_kernel(nb, lo_ref, frac_ref, win_ref, first_ref, vol_ref, base_ref, out_ref,
                   e_scr, f_scr, m_scr, acc):
    step = pl.program_id(0)

    @pl.when(step == 0)
    def _():
        fill_grid(base_ref, e_scr)
        v = lax.broadcasted_iota(jnp.int32, (LANES, VOX), 1)
        line = lax.broadcasted_iota(jnp.int32, (LANES, VOX), 0)
        q_of = (v // (BLK_SIDE * SUB)) * (BLK_SIDE // SUB) + (v % BLK_SIDE) // SUB
        m_scr[...] = jnp.where(q_of == line // 8, 1.0, 0.0).astype(jnp.bfloat16)
        zero = jnp.zeros((64, LANES), jnp.float32)

        def clear_angle(a, c):
            begin, end = merge_range(win_ref, a)
            begin = begin * (SPAN // 64)
            end = end * (SPAN // 64) + 1

            def clear(i, c):
                acc[pl.ds(aligned(a * TALL + i * 64, 64), 64), :] = zero
                return c

            return lax.fori_loop(begin, end, clear, c)

        lax.fori_loop(0, ANG_SUB, clear_angle, 0)

    def one(i, c):
        b = step * nb + i
        make_footprint(e_scr, f_scr, frac_ref, b)
        rounded = vol_ref[i].astype(jnp.bfloat16)
        spreadv = jnp.tile(rounded, (NQ, 1)) * m_scr[...]
        part = lax.dot_general(f_scr[...], spreadv, (((1,), (1,)), ((), ())),
                               preferred_element_type=jnp.float32)
        for a in range(ANG_SUB):
            at = pl.ds(a * TALL + PAD + lo_ref[b, a], R)
            acc[at, :] += part[a * R:(a + 1) * R, :]
        return c

    lax.fori_loop(0, nb, one, 0, unroll=2)

    @pl.when(step == pl.num_programs(0) - 1)
    def _():
        out_ref[...] = jnp.zeros_like(out_ref)
        span = SPAN
        lane_q = lax.broadcasted_iota(jnp.int32, (span, LANES), 1) // 8
        row_j = lax.broadcasted_iota(jnp.int32, (span, LANES), 0) % 16
        pick = lane_q == row_j

        def merge_angle(a, c):
            begin, end = merge_range(win_ref, a)

            def merge(i, c):
                k = i * span
                total = jnp.zeros((span, LANES), jnp.float32)
                for q in range(NQ):
                    src = a * TALL + PAD + k - first_ref[a, q]
                    total = jnp.where(lane_q == q, acc[pl.ds(src, span), :], total)
                for s in (64, 32, 16, 8):
                    total = total + pltpu.roll(total, s, 1)
                total = jnp.where(pick, total, 0.0)
                out = jnp.sum(total.reshape(span // 16, 16, LANES), axis=1)
                out_ref[pl.ds(aligned(a * (RAYS // 16) + i * 8, 8), 8), :] = out
                return c

            return lax.fori_loop(begin, end, merge, c)

        lax.fori_loop(0, ANG_SUB, merge_angle, 0)


def backward_kernel(nb, lo_ref, frac_ref, win_ref, first_ref, vol_ref, base_ref, res_ref, out_ref,
                    e_scr, f_scr, rb, dd):
    step = pl.program_id(0)

    @pl.when(step == 0)
    def _():
        fill_grid(base_ref, e_scr)
        span = SPAN
        lane_q = lax.broadcasted_iota(jnp.int32, (span, LANES), 1) // 8
        row_j = lax.broadcasted_iota(jnp.int32, (span, LANES), 0) % 16
        pick = lane_q == row_j
        fold = jnp.where(
            lax.broadcasted_iota(jnp.int32, (LANES, LANES), 0) % 8
            == lax.broadcasted_iota(jnp.int32, (LANES, LANES), 1) % 8, 1.0, 0.0).astype(jnp.bfloat16)

        def one_angle(a, c):
            begin = jnp.maximum((win_ref[0, a] - 64) // span, 0)
            end = jnp.minimum((win_ref[1, a] + 64 + span) // span + 1, RAYS // span)

            def widen(i, c):
                rows = res_ref[pl.ds(aligned(a * (RAYS // 16) + i * 8, 8), 8), :]
                wide = jnp.broadcast_to(rows[:, None, :], (8, 16, LANES)).reshape(span, LANES)
                wide = jnp.where(pick, wide, 0.0).astype(jnp.bfloat16)
                rb[pl.ds(aligned(PAD + i * span, 8), span), :] = jnp.dot(
                    wide, fold, preferred_element_type=jnp.float32)
                return c

            lax.fori_loop(begin, end, widen, 0)
            first = jnp.maximum(win_ref[0, a] // span, 0)
            last = jnp.minimum((win_ref[1, a] + 16) // span + 1, RAYS // span)

            def shift(i, c):
                k = i * span
                total = jnp.zeros((span, LANES), jnp.float32)
                for q in range(NQ):
                    src = PAD + k + first_ref[a, q]
                    total = jnp.where(lane_q == q, rb[pl.ds(src, span), :], total)
                dd[pl.ds(aligned(a * RAYS + k, span), span), :] = total
                return c

            lax.fori_loop(first, last, shift, 0)
            return c

        lax.fori_loop(0, ANG_SUB, one_angle, 0)

    width = SUB * BLK_SIDE
    group = BLK_SIDE // SUB
    lane = lax.broadcasted_iota(jnp.int32, (8, width), 1)
    col_group = (lane % BLK_SIDE) // SUB

    def one(i, c):
        b = step * nb + i
        make_footprint(e_scr, f_scr, frac_ref, b)
        rows = jnp.concatenate(
            [dd[pl.ds(a * RAYS + lo_ref[b, a], R), :] for a in range(ANG_SUB)], axis=0)
        turned = jnp.transpose(rows)
        ones = jnp.ones((8, ANG_SUB * R), jnp.float32)
        for g in range(group):
            lhs = jnp.concatenate([turned[g * 32:(g + 1) * 32], ones], axis=0).astype(jnp.bfloat16)
            at = slice(g * width, (g + 1) * width)
            part = jnp.dot(lhs, f_scr[:, at], preferred_element_type=jnp.float32)
            back = part[0:8]
            for j in range(1, group):
                back = jnp.where(col_group == j, part[j * 8:(j + 1) * 8], back)
            col_sum = part[32:40]
            out_ref[i, :, at] = jnp.maximum(vol_ref[i, :, at] + relax * back / col_sum, 0.0)
        return c

    lax.fori_loop(0, nb, one, 0, unroll=2)


def ray_sum_kernel(c_ref, s_ref, k_ref, out_ref):
    side = IMG_BLK * BLK_SIDE
    half = side * 0.5
    for u in range(c_ref.shape[0]):
        cs = c_ref[u] * (1.0 / spread)
        sn = s_ref[u] * (1.0 / spread)
        inv = 1.0 / cs
        ray = k_ref[u] * (1.0 / spread)

        def row(i, total):
            y = i.astype(jnp.float32) + (0.5 - half)
            w = ray - y * sn
            mid = jnp.floor(w * inv) + 0.5
            t0 = mid * cs - w
            for j in range(-2, 3):
                t = t0 + j * cs
                bump = jnp.maximum(1.0 - t * t, 0.0)
                total = total + jnp.where(jnp.abs(mid + j) < half, bump * bump, 0.0)
            return total

        out_ref[u] = lax.fori_loop(0, side, row, jnp.zeros(out_ref.shape[1:], jnp.float32), unroll=8)


def exchange_kernel(part_ref, mine_ref, on_ref, rs_ref, full_ref, own_ref,
                    half, inbox, sums, stage, gathered, send_sem, recv_sem,
                    pair_send, pair_recv, out_send, out_recv, back_send, back_recv):
    g, p = lax.axis_index("group"), lax.axis_index("patch")
    groups, pairs = inbox.shape[1], inbox.shape[0]
    n = groups * pairs
    parity, column = lax.rem(p, 2), p // 2
    me = column * groups + g
    partner = (g, column * 2 + 1 - parity)
    mesh_id = pl.DeviceIdType.MESH

    def peer(d):
        at = lax.rem(me + d, n)
        return at // groups, lax.rem(at, groups)

    barrier = pltpu.get_barrier_semaphore()
    pl.semaphore_signal(barrier, inc=1, device_id=partner, device_id_type=mesh_id)

    def greet(d, c):
        pc, pg = peer(d)
        pl.semaphore_signal(barrier, inc=1, device_id=(pg, pc * 2 + parity), device_id_type=mesh_id)
        return c

    lax.fori_loop(1, n, greet, 0)
    pl.semaphore_wait(barrier, n)

    swap = pltpu.make_async_remote_copy(
        src_ref=part_ref.at[:, 1 - parity], dst_ref=half, send_sem=pair_send, recv_sem=pair_recv,
        device_id=partner, device_id_type=mesh_id)
    swap.start()
    swap.wait()
    for i in range(pairs):
        sums[i] = part_ref[i, parity] + half[i]

    def to_owner(d):
        pc, pg = peer(d)
        return pltpu.make_async_remote_copy(
            src_ref=sums.at[pc, pg], dst_ref=inbox.at[column, g], send_sem=send_sem.at[d],
            recv_sem=recv_sem.at[d], device_id=(pg, pc * 2 + parity), device_id_type=mesh_id)

    def go(d, c):
        to_owner(d).start()
        return c

    def done(d, c):
        to_owner(d).wait()
        return c

    lax.fori_loop(1, n, go, 0)
    inbox[column, g] = sums[column, g]
    lax.fori_loop(1, n, done, 0)
    total = jnp.zeros(mine_ref.shape, jnp.float32)
    for i in range(pairs):
        for j in range(groups):
            total = total + inbox[i, j]
    residual = (mine_ref[...] - total / rs_ref[...]) * on_ref[...]
    own_ref[...] = residual
    stage[...] = residual.astype(jnp.bfloat16)

    def to_all(d):
        pc, pg = peer(d)
        return pltpu.make_async_remote_copy(
            src_ref=stage, dst_ref=gathered.at[column, parity, g], send_sem=out_send.at[d],
            recv_sem=out_recv.at[d], device_id=(pg, pc * 2 + parity), device_id_type=mesh_id)

    def go_all(d, c):
        to_all(d).start()
        return c

    def done_all(d, c):
        to_all(d).wait()
        return c

    lax.fori_loop(1, n, go_all, 0)
    gathered[column, parity, g] = stage[...]
    lax.fori_loop(1, n, done_all, 0)
    share = pltpu.make_async_remote_copy(
        src_ref=gathered.at[:, parity], dst_ref=gathered.at[:, parity], send_sem=back_send,
        recv_sem=back_recv, device_id=partner, device_id_type=mesh_id)
    share.start()
    share.wait()
    for i in range(pairs):
        full_ref[i] = gathered[i].astype(jnp.float32)


def exchange(partial, mine, on, rs, groups, patches):
    lines = mine.shape[0]
    pairs = patches // 2
    shape = (pairs, 2, groups, lines, LANES)
    n = pairs * groups
    dma = pltpu.SemaphoreType.DMA
    vmem = pl.BlockSpec(memory_space=pltpu.VMEM)
    full, own = pl.pallas_call(
        exchange_kernel,
        in_specs=[vmem] * 4,
        out_specs=[vmem] * 2,
        out_shape=[jax.ShapeDtypeStruct(shape, jnp.float32),
                   jax.ShapeDtypeStruct((lines, LANES), jnp.float32)],
        scratch_shapes=[pltpu.VMEM((pairs, groups, lines, LANES), jnp.float32),
                        pltpu.VMEM((pairs, groups, lines, LANES), jnp.float32),
                        pltpu.VMEM((pairs, groups, lines, LANES), jnp.float32),
                        pltpu.VMEM((lines, LANES), jnp.bfloat16),
                        pltpu.VMEM(shape, jnp.bfloat16),
                        dma((n,)), dma((n,)), dma, dma, dma((n,)), dma((n,)), dma, dma],
        compiler_params=pltpu.CompilerParams(collective_id=0, has_side_effects=True),
        name="exchange",
    )(partial.reshape(shape), mine, on, rs)
    return full.reshape(partial.shape), own


def smem():
    return pl.BlockSpec(memory_space=pltpu.SMEM)


def forward(volume, lo, frac, win, base, first):
    blocks, slices, _ = volume.shape
    nb = 8
    lines = ANG_SUB * RAYS // 16
    return pl.pallas_call(
        lambda *refs: forward_kernel(nb, *refs),
        grid=(blocks // nb,),
        in_specs=[smem(), smem(), smem(), smem(),
                  pl.BlockSpec((nb, slices, VOX), lambda i: (i, 0, 0)),
                  pl.BlockSpec((ANG_SUB, VOX), lambda i: (0, 0))],
        out_specs=pl.BlockSpec((lines, LANES), lambda i: (0, 0)),
        out_shape=jax.ShapeDtypeStruct((lines, LANES), jnp.float32),
        scratch_shapes=[pltpu.VMEM((ANG_SUB * R, VOX), jnp.float32),
                        pltpu.VMEM((ANG_SUB * R, VOX), jnp.bfloat16),
                        pltpu.VMEM((LANES, VOX), jnp.bfloat16),
                        pltpu.VMEM((ANG_SUB * TALL, LANES), jnp.float32)],
        compiler_params=pltpu.CompilerParams(vmem_limit_bytes=VMEM_LIMIT),
        name="forward",
    )(lo, frac, win, first, volume, base)


def backward(volume, residual, lo, frac, win, base, first):
    blocks, slices, _ = volume.shape
    nb = 8
    return pl.pallas_call(
        lambda *refs: backward_kernel(nb, *refs),
        grid=(blocks // nb,),
        in_specs=[smem(), smem(), smem(), smem(),
                  pl.BlockSpec((nb, slices, VOX), lambda i: (i, 0, 0)),
                  pl.BlockSpec((ANG_SUB, VOX), lambda i: (0, 0)),
                  pl.BlockSpec(residual.shape, lambda i: (0, 0))],
        out_specs=pl.BlockSpec((nb, slices, VOX), lambda i: (i, 0, 0)),
        out_shape=jax.ShapeDtypeStruct(volume.shape, jnp.float32),
        scratch_shapes=[pltpu.VMEM((ANG_SUB * R, VOX), jnp.float32),
                        pltpu.VMEM((ANG_SUB * R, VOX), jnp.bfloat16),
                        pltpu.VMEM((TALL, LANES), jnp.float32),
                        pltpu.VMEM((ANG_SUB * RAYS, LANES), jnp.float32)],
        compiler_params=pltpu.CompilerParams(vmem_limit_bytes=VMEM_LIMIT),
        name="backward",
    )(lo, frac, win, first, volume, base, residual)


def own_ray_sums(first_row, rows):
    count = rows * RAYS_TILE
    padded = -(-count // 1024) * 1024
    idx = jnp.minimum(jnp.arange(padded, dtype=jnp.int32), count - 1)
    row = first_row + idx // RAYS_TILE
    ray = ((row % NTILE) * RAYS_TILE + idx % RAYS_TILE).astype(jnp.float32) + (0.5 - RAYS * 0.5)
    angle = row // NTILE
    big, small = [], []
    for subset in range(SUBSETS):
        th = angles(subset)
        pairs = [sorted((math.cos(t), math.sin(t)), key=abs) for t in th]
        sign = jnp.zeros((padded,), jnp.float32)
        b, s = sign, sign
        for a in range(ANG_SUB):
            b = jnp.where(angle == a, np.float32(pairs[a][1]), b)
            s = jnp.where(angle == a, np.float32(pairs[a][0]), s)
        big.append(b)
        small.append(s)
    shape = (SUBSETS, padded // LANES, LANES)
    big = jnp.stack(big).reshape(shape)
    small = jnp.stack(small).reshape(shape)
    rays = jnp.broadcast_to(ray.reshape(1, padded // LANES, LANES), shape)
    sums = pl.pallas_call(
        ray_sum_kernel,
        out_shape=jax.ShapeDtypeStruct(shape, jnp.float32),
        name="raysum",
    )(big, small, rays)
    return sums.reshape(SUBSETS, padded)[:, :count]


def placing(place, subset):
    half = IMG_BLK * BLK_SIDE * 0.5
    x = (place % IMG_BLK).astype(jnp.float32) * BLK_SIDE + (BLK_SIDE * 0.5 - half)
    y = (place // IMG_BLK).astype(jnp.float32) * BLK_SIDE + (BLK_SIDE * 0.5 - half)
    cosine = np.cos(np.array(angles(subset))).astype(np.float32)
    sine = np.sin(np.array(angles(subset))).astype(np.float32)
    z = x[:, None] * cosine + y[:, None] * sine + (RAYS * 0.5 - 0.5)
    low = jnp.floor(z)
    lo = low.astype(jnp.int32)
    win = jnp.stack([jnp.min(lo, axis=0), jnp.max(lo, axis=0)])
    return lo, (z - low) * (1.0 / spread), win


def shards(volume, block_place, measured, live_rays):
    groups = lax.axis_size("group")
    patches = lax.axis_size("patch")
    group_index = lax.axis_index("group")
    patch_index = lax.axis_index("patch")
    slices = volume.shape[1]
    slab_rows = ANG_SUB * NTILE // patches
    rows = slab_rows // groups
    first_row = patch_index * slab_rows + group_index * rows
    lines = rows * RAYS_TILE * slices // LANES
    per = LANES // slices
    sums = own_ray_sums(first_row, rows)
    estimate = volume
    own_residual = None
    for subset in range(SUBSETS):
        base, first = geometry(subset)
        lo, frac, win = placing(block_place, subset)
        partial = forward(estimate, lo, frac, win, base, first)
        mine = lax.dynamic_slice_in_dim(measured[subset], group_index * rows, rows, 0)
        live = lax.dynamic_slice_in_dim(live_rays[subset], first_row, rows, 0)
        on = jnp.arange(RAYS_TILE, dtype=jnp.int32)[None, :] < live[:, None]
        on = jnp.broadcast_to(on[:, :, None], (rows, RAYS_TILE, slices)).reshape(lines, LANES)
        rs = jnp.maximum(sums[subset], 1.0).reshape(lines, per, 1)
        rs = jnp.broadcast_to(rs, (lines, per, slices)).reshape(lines, LANES)
        full, own = exchange(partial, mine.reshape(lines, LANES), on.astype(jnp.float32), rs, groups, patches)
        own_residual = own.reshape(rows, RAYS_TILE * slices)
        estimate = backward(estimate, full, lo, frac, win, base, first)
    return (estimate, own_residual[None])


def solution(mesh):
    return jax.shard_map(
        shards,
        mesh=mesh,
        in_specs=(
            P(("group", "patch"), None, None),
            P(("group", "patch")),
            P(None, "patch", None),
            P(),
        ),
        out_specs=(P(("group", "patch"), None, None), P("group", "patch", None)),
        check_vma=False,
    )
```

```python
import math

import jax
import jax.numpy as jnp
import numpy as np
from jax import lax
from jax.experimental import pallas as pl
from jax.experimental.pallas import tpu as pltpu
from jax.sharding import PartitionSpec as P

IMG_BLK = 64
BLK_SIDE = 32
RAYS_TILE = 48
NTILE = 64
ANG_SUB = 8
SUBSETS = 2

spread = 1.5
relax = 0.9

SUB = 8
NQ = (BLK_SIDE // SUB) ** 2
R = 16
VOX = BLK_SIDE * BLK_SIDE
RAYS = NTILE * RAYS_TILE
LANES = 128
PAD = 32
SPAN = 128
TALL = RAYS + SPAN
VMEM_LIMIT = 60 * 1024 * 1024


def angles(subset):
    return [math.pi * (a * SUBSETS + subset) / (ANG_SUB * SUBSETS) for a in range(ANG_SUB)]


def geometry(subset):
    v = np.arange(VOX)
    col = (v % BLK_SIDE) + 0.5 - BLK_SIDE / 2
    row = (v // BLK_SIDE) + 0.5 - BLK_SIDE / 2
    q_of = (v // BLK_SIDE // SUB) * (BLK_SIDE // SUB) + (v % BLK_SIDE) // SUB
    base = np.zeros((ANG_SUB, VOX), np.float64)
    first = np.zeros((ANG_SUB, NQ), np.int64)
    for a, theta in enumerate(angles(subset)):
        off = col * math.cos(theta) + row * math.sin(theta)
        for q in range(NQ):
            mine = q_of == q
            first[a, q] = math.floor(off[mine].min() - spread)
            base[a, mine] = off[mine] - first[a, q]
    return base.astype(np.float32), first.astype(np.int32)


def fill_grid(base_ref, e_scr):
    ray = lax.broadcasted_iota(jnp.int32, (R, VOX), 0).astype(jnp.float32)
    for a in range(ANG_SUB):
        e_scr[a * R:(a + 1) * R, :] = (base_ref[a:a + 1, :] - ray) * (1.0 / spread)


def make_footprint(e_scr, f_scr, frac_ref, b):
    for a in range(ANG_SUB):
        t = e_scr[a * R:(a + 1) * R, :] + frac_ref[b, a]
        bump = jnp.maximum(1.0 - t * t, 0.0)
        f_scr[a * R:(a + 1) * R, :] = (bump * bump).astype(jnp.bfloat16)


def aligned(x, m):
    return pl.multiple_of(x, m)


def forward_kernel(nb, lo_ref, frac_ref, win_ref, first_ref, vol_ref, base_ref, out_ref,
                   e_scr, f_even, f_odd, m_scr, acc):
    f_bufs = (f_even, f_odd)
    step = pl.program_id(0)

    @pl.when(step == 0)
    def _():
        fill_grid(base_ref, e_scr)
        v = lax.broadcasted_iota(jnp.int32, (LANES, VOX), 1)
        line = lax.broadcasted_iota(jnp.int32, (LANES, VOX), 0)
        q_of = (v // (BLK_SIDE * SUB)) * (BLK_SIDE // SUB) + (v % BLK_SIDE) // SUB
        m_scr[...] = jnp.where(q_of == line // 8, 1.0, 0.0).astype(jnp.bfloat16)
        zero = jnp.zeros((SPAN, LANES), jnp.float32)

        def clear_angle(a, c):
            def clear(i, c):
                @pl.when(win_ref[1, a * (TALL // SPAN) + i] > 0)
                def _():
                    acc[pl.ds(aligned(a * TALL + i * SPAN, SPAN), SPAN), :] = zero
                return c

            return lax.fori_loop(0, TALL // SPAN, clear, c)

        lax.fori_loop(0, ANG_SUB, clear_angle, 0)

    for i in range(nb):
        b = step * nb + i
        f_scr = f_bufs[i % 2]
        make_footprint(e_scr, f_scr, frac_ref, b)
        rounded = vol_ref[i].astype(jnp.bfloat16)
        spreadv = jnp.tile(rounded, (NQ, 1)) * m_scr[...]
        part = lax.dot_general(f_scr[...], spreadv, (((1,), (1,)), ((), ())),
                               preferred_element_type=jnp.float32)
        for a in range(ANG_SUB):
            at = pl.ds(a * TALL + PAD + lo_ref[b, a], R)
            acc[at, :] += part[a * R:(a + 1) * R, :]

    @pl.when(step == pl.num_programs(0) - 1)
    def _():
        out_ref[...] = jnp.zeros_like(out_ref)
        span = SPAN
        lane_q = lax.broadcasted_iota(jnp.int32, (span, LANES), 1) // 8
        row_j = lax.broadcasted_iota(jnp.int32, (span, LANES), 0) % 16
        pick = lane_q == row_j

        def merge_angle(a, c):
            def merge(i, c):
                @pl.when(win_ref[0, a * (TALL // SPAN) + i] > 0)
                def _():
                    k = i * span
                    total = jnp.zeros((span, LANES), jnp.float32)
                    for q in range(NQ):
                        src = a * TALL + PAD + k - first_ref[a, q]
                        total = jnp.where(lane_q == q, acc[pl.ds(src, span), :], total)
                    for s in (64, 32, 16, 8):
                        total = total + pltpu.roll(total, s, 1)
                    total = jnp.where(pick, total, 0.0)
                    out = jnp.sum(total.reshape(span // 16, 16, LANES), axis=1)
                    out_ref[pl.ds(aligned(a * (RAYS // 16) + i * 8, 8), 8), :] = out
                return c

            return lax.fori_loop(0, RAYS // span, merge, c)

        lax.fori_loop(0, ANG_SUB, merge_angle, 0)


def backward_kernel(nb, lo_ref, frac_ref, win_ref, first_ref, vol_ref, base_ref, res_ref, out_ref,
                    e_scr, f_even, f_odd, rb, dd):
    f_bufs = (f_even, f_odd)
    step = pl.program_id(0)

    @pl.when(step == 0)
    def _():
        fill_grid(base_ref, e_scr)
        span = SPAN
        lane_q = lax.broadcasted_iota(jnp.int32, (span, LANES), 1) // 8
        row_j = lax.broadcasted_iota(jnp.int32, (span, LANES), 0) % 16
        pick = lane_q == row_j
        fold = jnp.where(
            lax.broadcasted_iota(jnp.int32, (LANES, LANES), 0) % 8
            == lax.broadcasted_iota(jnp.int32, (LANES, LANES), 1) % 8, 1.0, 0.0).astype(jnp.bfloat16)

        def one_angle(a, c):
            def widen(i, c):
                @pl.when(win_ref[0, a * (TALL // SPAN) + i] > 0)
                def _():
                    rows = res_ref[pl.ds(aligned(a * (RAYS // 16) + i * 8, 8), 8), :]
                    wide = jnp.broadcast_to(rows[:, None, :], (8, 16, LANES)).reshape(span, LANES)
                    wide = jnp.where(pick, wide, 0.0).astype(jnp.bfloat16)
                    rb[pl.ds(aligned(PAD + i * span, 8), span), :] = jnp.dot(
                        wide, fold, preferred_element_type=jnp.float32)
                return c

            lax.fori_loop(0, RAYS // span, widen, 0)

            def shift(i, c):
                @pl.when(win_ref[0, a * (TALL // SPAN) + i] > 0)
                def _():
                    k = i * span
                    total = jnp.zeros((span, LANES), jnp.float32)
                    for q in range(NQ):
                        src = PAD + k + first_ref[a, q]
                        total = jnp.where(lane_q == q, rb[pl.ds(src, span), :], total)
                    dd[pl.ds(aligned(a * RAYS + k, span), span), :] = total
                return c

            lax.fori_loop(0, RAYS // span, shift, 0)
            return c

        lax.fori_loop(0, ANG_SUB, one_angle, 0)

    width = SUB * BLK_SIDE
    group = BLK_SIDE // SUB
    lane = lax.broadcasted_iota(jnp.int32, (8, width), 1)
    col_group = (lane % BLK_SIDE) // SUB

    for i in range(nb):
        b = step * nb + i
        f_scr = f_bufs[i % 2]
        make_footprint(e_scr, f_scr, frac_ref, b)
        rows = jnp.concatenate(
            [dd[pl.ds(a * RAYS + lo_ref[b, a], R), :] for a in range(ANG_SUB)], axis=0)
        turned = jnp.transpose(rows)
        ones = jnp.ones((8, ANG_SUB * R), jnp.float32)
        for g in range(group):
            lhs = jnp.concatenate([turned[g * 32:(g + 1) * 32], ones], axis=0).astype(jnp.bfloat16)
            at = slice(g * width, (g + 1) * width)
            part = jnp.dot(lhs, f_scr[:, at], preferred_element_type=jnp.float32)
            back = part[0:8]
            for j in range(1, group):
                back = jnp.where(col_group == j, part[j * 8:(j + 1) * 8], back)
            col_sum = part[32:40]
            out_ref[i, :, at] = jnp.maximum(vol_ref[i, :, at] + relax * back / col_sum, 0.0)


def ray_sum_kernel(c_ref, s_ref, k_ref, out_ref):
    side = IMG_BLK * BLK_SIDE
    half = side * 0.5
    for u in range(c_ref.shape[0]):
        cs = c_ref[u] * (1.0 / spread)
        sn = s_ref[u] * (1.0 / spread)
        inv = 1.0 / cs
        ray = k_ref[u] * (1.0 / spread)

        def row(i, total):
            y = i.astype(jnp.float32) + (0.5 - half)
            w = ray - y * sn
            mid = jnp.clip(jnp.floor(w * inv) + 0.5, 2.5 - half, half - 2.5)
            t0 = mid * cs - w
            for t in (t0 - 2 * cs, t0 - cs, t0, t0 + cs, t0 + 2 * cs):
                bump = jnp.maximum(1.0 - t * t, 0.0)
                total = total + bump * bump
            return total

        out_ref[u] = lax.fori_loop(0, side, row, jnp.zeros(out_ref.shape[1:], jnp.float32), unroll=8)


def exchange_kernel(part_ref, mine_ref, on_ref, rs_ref, full_ref, own_ref,
                    half, inbox, sums, stage, gathered, send_sem, recv_sem,
                    pair_send, pair_recv, out_send, out_recv, back_send, back_recv):
    g, p = lax.axis_index("group"), lax.axis_index("patch")
    groups, pairs = inbox.shape[1], inbox.shape[0]
    n = groups * pairs
    parity, column = lax.rem(p, 2), p // 2
    me = column * groups + g
    partner = (g, column * 2 + 1 - parity)
    mesh_id = pl.DeviceIdType.MESH

    def peer(d):
        at = lax.rem(me + d, n)
        return at // groups, lax.rem(at, groups)

    barrier = pltpu.get_barrier_semaphore()
    pl.semaphore_signal(barrier, inc=1, device_id=partner, device_id_type=mesh_id)

    def greet(d, c):
        pc, pg = peer(d)
        pl.semaphore_signal(barrier, inc=1, device_id=(pg, pc * 2 + parity), device_id_type=mesh_id)
        return c

    lax.fori_loop(1, n, greet, 0)
    pl.semaphore_wait(barrier, n)

    swap = pltpu.make_async_remote_copy(
        src_ref=part_ref.at[:, 1 - parity], dst_ref=half, send_sem=pair_send, recv_sem=pair_recv,
        device_id=partner, device_id_type=mesh_id)
    swap.start()
    swap.wait()
    for i in range(pairs):
        sums[i] = part_ref[i, parity] + half[i]

    def to_owner(d):
        pc, pg = peer(d)
        return pltpu.make_async_remote_copy(
            src_ref=sums.at[pc, pg], dst_ref=inbox.at[column, g], send_sem=send_sem.at[d],
            recv_sem=recv_sem.at[d], device_id=(pg, pc * 2 + parity), device_id_type=mesh_id)

    def go(d, c):
        to_owner(d).start()
        return c

    def done(d, c):
        to_owner(d).wait()
        return c

    lax.fori_loop(1, n, go, 0)
    inbox[column, g] = sums[column, g]
    lax.fori_loop(1, n, done, 0)
    total = jnp.zeros(mine_ref.shape, jnp.float32)
    for i in range(pairs):
        for j in range(groups):
            total = total + inbox[i, j]
    residual = (mine_ref[...] - total / rs_ref[...]) * on_ref[...]
    own_ref[...] = residual
    stage[...] = residual.astype(jnp.bfloat16)

    def to_all(d):
        pc, pg = peer(d)
        return pltpu.make_async_remote_copy(
            src_ref=stage, dst_ref=gathered.at[column, parity, g], send_sem=out_send.at[d],
            recv_sem=out_recv.at[d], device_id=(pg, pc * 2 + parity), device_id_type=mesh_id)

    def go_all(d, c):
        to_all(d).start()
        return c

    def done_all(d, c):
        to_all(d).wait()
        return c

    lax.fori_loop(1, n, go_all, 0)
    gathered[column, parity, g] = stage[...]
    lax.fori_loop(1, n, done_all, 0)
    share = pltpu.make_async_remote_copy(
        src_ref=gathered.at[:, parity], dst_ref=gathered.at[:, parity], send_sem=back_send,
        recv_sem=back_recv, device_id=partner, device_id_type=mesh_id)
    share.start()
    share.wait()
    for i in range(pairs):
        full_ref[i] = gathered[i].astype(jnp.float32)


def exchange(partial, mine, on, rs, groups, patches):
    lines = mine.shape[0]
    pairs = patches // 2
    shape = (pairs, 2, groups, lines, LANES)
    n = pairs * groups
    dma = pltpu.SemaphoreType.DMA
    vmem = pl.BlockSpec(memory_space=pltpu.VMEM)
    full, own = pl.pallas_call(
        exchange_kernel,
        in_specs=[vmem] * 4,
        out_specs=[vmem] * 2,
        out_shape=[jax.ShapeDtypeStruct(shape, jnp.float32),
                   jax.ShapeDtypeStruct((lines, LANES), jnp.float32)],
        scratch_shapes=[pltpu.VMEM((pairs, groups, lines, LANES), jnp.float32),
                        pltpu.VMEM((pairs, groups, lines, LANES), jnp.float32),
                        pltpu.VMEM((pairs, groups, lines, LANES), jnp.float32),
                        pltpu.VMEM((lines, LANES), jnp.bfloat16),
                        pltpu.VMEM(shape, jnp.bfloat16),
                        dma((n,)), dma((n,)), dma, dma, dma((n,)), dma((n,)), dma, dma],
        compiler_params=pltpu.CompilerParams(collective_id=0, has_side_effects=True),
        name="exchange",
    )(partial.reshape(shape), mine, on, rs)
    return full.reshape(partial.shape), own


def smem():
    return pl.BlockSpec(memory_space=pltpu.SMEM)


def forward(volume, lo, frac, win, base, first):
    blocks, slices, _ = volume.shape
    nb = 8
    lines = ANG_SUB * RAYS // 16
    return pl.pallas_call(
        lambda *refs: forward_kernel(nb, *refs),
        grid=(blocks // nb,),
        in_specs=[smem(), smem(), smem(), smem(),
                  pl.BlockSpec((nb, slices, VOX), lambda i: (i, 0, 0)),
                  pl.BlockSpec((ANG_SUB, VOX), lambda i: (0, 0))],
        out_specs=pl.BlockSpec((lines, LANES), lambda i: (0, 0)),
        out_shape=jax.ShapeDtypeStruct((lines, LANES), jnp.float32),
        scratch_shapes=[pltpu.VMEM((ANG_SUB * R, VOX), jnp.float32),
                        pltpu.VMEM((ANG_SUB * R, VOX), jnp.bfloat16),
                        pltpu.VMEM((ANG_SUB * R, VOX), jnp.bfloat16),
                        pltpu.VMEM((LANES, VOX), jnp.bfloat16),
                        pltpu.VMEM((ANG_SUB * TALL, LANES), jnp.float32)],
        compiler_params=pltpu.CompilerParams(vmem_limit_bytes=VMEM_LIMIT),
        name="forward",
    )(lo, frac, win, first, volume, base)


def backward(volume, residual, lo, frac, win, base, first):
    blocks, slices, _ = volume.shape
    nb = 8
    return pl.pallas_call(
        lambda *refs: backward_kernel(nb, *refs),
        grid=(blocks // nb,),
        in_specs=[smem(), smem(), smem(), smem(),
                  pl.BlockSpec((nb, slices, VOX), lambda i: (i, 0, 0)),
                  pl.BlockSpec((ANG_SUB, VOX), lambda i: (0, 0)),
                  pl.BlockSpec(residual.shape, lambda i: (0, 0))],
        out_specs=pl.BlockSpec((nb, slices, VOX), lambda i: (i, 0, 0)),
        out_shape=jax.ShapeDtypeStruct(volume.shape, jnp.float32),
        scratch_shapes=[pltpu.VMEM((ANG_SUB * R, VOX), jnp.float32),
                        pltpu.VMEM((ANG_SUB * R, VOX), jnp.bfloat16),
                        pltpu.VMEM((ANG_SUB * R, VOX), jnp.bfloat16),
                        pltpu.VMEM((TALL, LANES), jnp.float32),
                        pltpu.VMEM((ANG_SUB * RAYS, LANES), jnp.float32)],
        compiler_params=pltpu.CompilerParams(vmem_limit_bytes=VMEM_LIMIT),
        name="backward",
    )(lo, frac, win, first, volume, base, residual)


def own_ray_sums(first_row, rows):
    count = rows * RAYS_TILE
    padded = -(-count // 1024) * 1024
    idx = jnp.minimum(jnp.arange(padded, dtype=jnp.int32), count - 1)
    row = first_row + idx // RAYS_TILE
    ray = ((row % NTILE) * RAYS_TILE + idx % RAYS_TILE).astype(jnp.float32) + (0.5 - RAYS * 0.5)
    angle = row // NTILE
    big, small = [], []
    for subset in range(SUBSETS):
        th = angles(subset)
        pairs = [sorted((math.cos(t), math.sin(t)), key=abs) for t in th]
        sign = jnp.zeros((padded,), jnp.float32)
        b, s = sign, sign
        for a in range(ANG_SUB):
            b = jnp.where(angle == a, np.float32(pairs[a][1]), b)
            s = jnp.where(angle == a, np.float32(pairs[a][0]), s)
        big.append(b)
        small.append(s)
    shape = (SUBSETS, padded // LANES, LANES)
    big = jnp.stack(big).reshape(shape)
    small = jnp.stack(small).reshape(shape)
    rays = jnp.broadcast_to(ray.reshape(1, padded // LANES, LANES), shape)
    sums = pl.pallas_call(
        ray_sum_kernel,
        out_shape=jax.ShapeDtypeStruct(shape, jnp.float32),
        name="raysum",
    )(big, small, rays)
    return sums.reshape(SUBSETS, padded)[:, :count]


def placing(place, subset):
    half = IMG_BLK * BLK_SIDE * 0.5
    x = (place % IMG_BLK).astype(jnp.float32) * BLK_SIDE + (BLK_SIDE * 0.5 - half)
    y = (place // IMG_BLK).astype(jnp.float32) * BLK_SIDE + (BLK_SIDE * 0.5 - half)
    cosine = np.cos(np.array(angles(subset))).astype(np.float32)
    sine = np.sin(np.array(angles(subset))).astype(np.float32)
    z = x[:, None] * cosine + y[:, None] * sine + (RAYS * 0.5 - 0.5)
    low = jnp.floor(z)
    lo = low.astype(jnp.int32)
    tile = jnp.arange(TALL // SPAN, dtype=jnp.int32)
    touched = jnp.any(((lo - PAD) // SPAN)[:, :, None] == tile, axis=0)
    touched |= jnp.any(((lo + R + PAD) // SPAN)[:, :, None] == tile, axis=0)
    cleared = touched | jnp.pad(touched[:, :-1], ((0, 0), (1, 0)))
    win = jnp.stack([touched.reshape(-1), cleared.reshape(-1)]).astype(jnp.int32)
    return lo, (z - low) * (1.0 / spread), win


def shards(volume, block_place, measured, live_rays):
    groups = lax.axis_size("group")
    patches = lax.axis_size("patch")
    group_index = lax.axis_index("group")
    patch_index = lax.axis_index("patch")
    slices = volume.shape[1]
    slab_rows = ANG_SUB * NTILE // patches
    rows = slab_rows // groups
    first_row = patch_index * slab_rows + group_index * rows
    lines = rows * RAYS_TILE * slices // LANES
    per = LANES // slices
    sums = own_ray_sums(first_row, rows)
    estimate = volume
    own_residual = None
    for subset in range(SUBSETS):
        base, first = geometry(subset)
        lo, frac, win = placing(block_place, subset)
        partial = forward(estimate, lo, frac, win, base, first)
        mine = lax.dynamic_slice_in_dim(measured[subset], group_index * rows, rows, 0)
        live = lax.dynamic_slice_in_dim(live_rays[subset], first_row, rows, 0)
        on = jnp.arange(RAYS_TILE, dtype=jnp.int32)[None, :] < live[:, None]
        on = jnp.broadcast_to(on[:, :, None], (rows, RAYS_TILE, slices)).reshape(lines, LANES)
        rs = jnp.maximum(sums[subset], 1.0).reshape(lines, per, 1)
        rs = jnp.broadcast_to(rs, (lines, per, slices)).reshape(lines, LANES)
        full, own = exchange(partial, mine.reshape(lines, LANES), on.astype(jnp.float32), rs, groups, patches)
        own_residual = own.reshape(rows, RAYS_TILE * slices)
        estimate = backward(estimate, full, lo, frac, win, base, first)
    return (estimate, own_residual[None])


def solution(mesh):
    return jax.shard_map(
        shards,
        mesh=mesh,
        in_specs=(
            P(("group", "patch"), None, None),
            P(("group", "patch")),
            P(None, "patch", None),
            P(),
        ),
        out_specs=(P(("group", "patch"), None, None), P("group", "patch", None)),
        check_vma=False,
    )
```

```python
import math

import jax
import jax.numpy as jnp
import numpy as np
from jax import lax
from jax.experimental import pallas as pl
from jax.experimental.pallas import tpu as pltpu
from jax.sharding import PartitionSpec as P

IMG_BLK = 64
BLK_SIDE = 32
RAYS_TILE = 48
NTILE = 64
ANG_SUB = 8
SUBSETS = 2

spread = 1.5
relax = 0.9

SUB = 8
NQ = (BLK_SIDE // SUB) ** 2
R = 16
VOX = BLK_SIDE * BLK_SIDE
RAYS = NTILE * RAYS_TILE
LANES = 128
PAD = 32
SPAN = 128
TALL = RAYS + SPAN
VMEM_LIMIT = 60 * 1024 * 1024


def angles(subset):
    return [math.pi * (a * SUBSETS + subset) / (ANG_SUB * SUBSETS) for a in range(ANG_SUB)]


def geometry(subset):
    v = np.arange(VOX)
    col = (v % BLK_SIDE) + 0.5 - BLK_SIDE / 2
    row = (v // BLK_SIDE) + 0.5 - BLK_SIDE / 2
    q_of = (v // BLK_SIDE // SUB) * (BLK_SIDE // SUB) + (v % BLK_SIDE) // SUB
    base = np.zeros((ANG_SUB, VOX), np.float64)
    first = np.zeros((ANG_SUB, NQ), np.int64)
    for a, theta in enumerate(angles(subset)):
        off = col * math.cos(theta) + row * math.sin(theta)
        for q in range(NQ):
            mine = q_of == q
            first[a, q] = math.floor(off[mine].min() - spread)
            base[a, mine] = off[mine] - first[a, q]
    return base.astype(np.float32), first.astype(np.int32)


def fill_grid(base_ref, e_scr):
    ray = lax.broadcasted_iota(jnp.int32, (R, VOX), 0).astype(jnp.float32)
    for a in range(ANG_SUB):
        e_scr[a * R:(a + 1) * R, :] = (base_ref[a:a + 1, :] - ray) * (1.0 / spread)


def make_footprint(e_scr, f_scr, frac_ref, b):
    for a in range(ANG_SUB):
        t = e_scr[a * R:(a + 1) * R, :] + frac_ref[b, a]
        bump = jnp.maximum(1.0 - t * t, 0.0)
        f_scr[a * R:(a + 1) * R, :] = (bump * bump).astype(jnp.bfloat16)


def aligned(x, m):
    return pl.multiple_of(x, m)


def forward_kernel(nb, lo_ref, frac_ref, win_ref, first_ref, vol_ref, base_ref, out_ref, foot_ref,
                   e_scr, m_scr, acc):
    step = pl.program_id(0)

    @pl.when(step == 0)
    def _():
        fill_grid(base_ref, e_scr)
        v = lax.broadcasted_iota(jnp.int32, (LANES, VOX), 1)
        line = lax.broadcasted_iota(jnp.int32, (LANES, VOX), 0)
        q_of = (v // (BLK_SIDE * SUB)) * (BLK_SIDE // SUB) + (v % BLK_SIDE) // SUB
        m_scr[...] = jnp.where(q_of == line // 8, 1.0, 0.0).astype(jnp.bfloat16)
        zero = jnp.zeros((SPAN, LANES), jnp.float32)

        def clear_angle(a, c):
            def clear(i, c):
                @pl.when(win_ref[1, a * (TALL // SPAN) + i] > 0)
                def _():
                    acc[pl.ds(aligned(a * TALL + i * SPAN, SPAN), SPAN), :] = zero
                return c

            return lax.fori_loop(0, TALL // SPAN, clear, c)

        lax.fori_loop(0, ANG_SUB, clear_angle, 0)

    for i in range(nb):
        b = step * nb + i
        make_footprint(e_scr, foot_ref.at[i], frac_ref, b)
        rounded = vol_ref[i].astype(jnp.bfloat16)
        spreadv = jnp.tile(rounded, (NQ, 1)) * m_scr[...]
        part = lax.dot_general(foot_ref[i], spreadv, (((1,), (1,)), ((), ())),
                               preferred_element_type=jnp.float32)
        for a in range(ANG_SUB):
            at = pl.ds(a * TALL + PAD + lo_ref[b, a], R)
            acc[at, :] += part[a * R:(a + 1) * R, :]

    @pl.when(step == pl.num_programs(0) - 1)
    def _():
        out_ref[...] = jnp.zeros_like(out_ref)
        span = SPAN
        lane_q = lax.broadcasted_iota(jnp.int32, (span, LANES), 1) // 8
        row_j = lax.broadcasted_iota(jnp.int32, (span, LANES), 0) % 16
        pick = lane_q == row_j

        def merge_angle(a, c):
            def merge(i, c):
                @pl.when(win_ref[0, a * (TALL // SPAN) + i] > 0)
                def _():
                    k = i * span
                    total = jnp.zeros((span, LANES), jnp.float32)
                    for q in range(NQ):
                        src = a * TALL + PAD + k - first_ref[a, q]
                        total = jnp.where(lane_q == q, acc[pl.ds(src, span), :], total)
                    for s in (64, 32, 16, 8):
                        total = total + pltpu.roll(total, s, 1)
                    total = jnp.where(pick, total, 0.0)
                    out = jnp.sum(total.reshape(span // 16, 16, LANES), axis=1)
                    out_ref[pl.ds(aligned(a * (RAYS // 16) + i * 8, 8), 8), :] = out
                return c

            return lax.fori_loop(0, RAYS // span, merge, c)

        lax.fori_loop(0, ANG_SUB, merge_angle, 0)


def backward_kernel(nb, lo_ref, win_ref, first_ref, vol_ref, foot_ref, res_ref, out_ref, rb, dd):
    step = pl.program_id(0)

    @pl.when(step == 0)
    def _():
        span = SPAN
        lane_q = lax.broadcasted_iota(jnp.int32, (span, LANES), 1) // 8
        row_j = lax.broadcasted_iota(jnp.int32, (span, LANES), 0) % 16
        pick = lane_q == row_j
        fold = jnp.where(
            lax.broadcasted_iota(jnp.int32, (LANES, LANES), 0) % 8
            == lax.broadcasted_iota(jnp.int32, (LANES, LANES), 1) % 8, 1.0, 0.0).astype(jnp.bfloat16)

        def one_angle(a, c):
            def widen(i, c):
                @pl.when(win_ref[0, a * (TALL // SPAN) + i] > 0)
                def _():
                    rows = res_ref[pl.ds(aligned(a * (RAYS // 16) + i * 8, 8), 8), :]
                    wide = jnp.broadcast_to(rows[:, None, :], (8, 16, LANES)).reshape(span, LANES)
                    wide = jnp.where(pick, wide, 0.0).astype(jnp.bfloat16)
                    rb[pl.ds(aligned(PAD + i * span, 8), span), :] = jnp.dot(
                        wide, fold, preferred_element_type=jnp.float32)
                return c

            lax.fori_loop(0, RAYS // span, widen, 0)

            def shift(i, c):
                @pl.when(win_ref[0, a * (TALL // SPAN) + i] > 0)
                def _():
                    k = i * span
                    total = jnp.zeros((span, LANES), jnp.float32)
                    for q in range(NQ):
                        src = PAD + k + first_ref[a, q]
                        total = jnp.where(lane_q == q, rb[pl.ds(src, span), :], total)
                    dd[pl.ds(aligned(a * RAYS + k, span), span), :] = total
                return c

            lax.fori_loop(0, RAYS // span, shift, 0)
            return c

        lax.fori_loop(0, ANG_SUB, one_angle, 0)

    width = SUB * BLK_SIDE
    group = BLK_SIDE // SUB
    lane = lax.broadcasted_iota(jnp.int32, (8, width), 1)
    col_group = (lane % BLK_SIDE) // SUB

    for i in range(nb):
        b = step * nb + i
        rows = jnp.concatenate(
            [dd[pl.ds(a * RAYS + lo_ref[b, a], R), :] for a in range(ANG_SUB)], axis=0)
        turned = jnp.transpose(rows)
        ones = jnp.ones((8, ANG_SUB * R), jnp.float32)
        for g in range(group):
            lhs = jnp.concatenate([turned[g * 32:(g + 1) * 32], ones], axis=0).astype(jnp.bfloat16)
            at = slice(g * width, (g + 1) * width)
            part = jnp.dot(lhs, foot_ref[i, :, at], preferred_element_type=jnp.float32)
            back = part[0:8]
            for j in range(1, group):
                back = jnp.where(col_group == j, part[j * 8:(j + 1) * 8], back)
            col_sum = part[32:40]
            out_ref[i, :, at] = jnp.maximum(vol_ref[i, :, at] + relax * back / col_sum, 0.0)


def ray_sum_kernel(c_ref, s_ref, k_ref, out_ref):
    side = IMG_BLK * BLK_SIDE
    half = side * 0.5
    for u in range(c_ref.shape[0]):
        cs = c_ref[u] * (1.0 / spread)
        sn = s_ref[u] * (1.0 / spread)
        inv = 1.0 / cs
        ray = k_ref[u] * (1.0 / spread)

        def row(i, total):
            y = i.astype(jnp.float32) + (0.5 - half)
            w = ray - y * sn
            mid = jnp.clip(jnp.floor(w * inv) + 0.5, 2.5 - half, half - 2.5)
            t0 = mid * cs - w
            for t in (t0 - 2 * cs, t0 - cs, t0, t0 + cs, t0 + 2 * cs):
                bump = jnp.maximum(1.0 - t * t, 0.0)
                total = total + bump * bump
            return total

        out_ref[u] = lax.fori_loop(0, side, row, jnp.zeros(out_ref.shape[1:], jnp.float32), unroll=8)


def exchange_kernel(part_ref, mine_ref, on_ref, rs_ref, full_ref, own_ref,
                    half, inbox, sums, stage, gathered, send_sem, recv_sem,
                    pair_send, pair_recv, out_send, out_recv, back_send, back_recv):
    g, p = lax.axis_index("group"), lax.axis_index("patch")
    groups, pairs = inbox.shape[1], inbox.shape[0]
    n = groups * pairs
    parity, column = lax.rem(p, 2), p // 2
    me = column * groups + g
    partner = (g, column * 2 + 1 - parity)
    mesh_id = pl.DeviceIdType.MESH

    def peer(d):
        at = lax.rem(me + d, n)
        return at // groups, lax.rem(at, groups)

    barrier = pltpu.get_barrier_semaphore()
    pl.semaphore_signal(barrier, inc=1, device_id=partner, device_id_type=mesh_id)

    def greet(d, c):
        pc, pg = peer(d)
        pl.semaphore_signal(barrier, inc=1, device_id=(pg, pc * 2 + parity), device_id_type=mesh_id)
        return c

    lax.fori_loop(1, n, greet, 0)
    pl.semaphore_wait(barrier, n)

    swap = pltpu.make_async_remote_copy(
        src_ref=part_ref.at[:, 1 - parity], dst_ref=half, send_sem=pair_send, recv_sem=pair_recv,
        device_id=partner, device_id_type=mesh_id)
    swap.start()
    swap.wait()
    for i in range(pairs):
        sums[i] = part_ref[i, parity] + half[i]

    def to_owner(d):
        pc, pg = peer(d)
        return pltpu.make_async_remote_copy(
            src_ref=sums.at[pc, pg], dst_ref=inbox.at[column, g], send_sem=send_sem.at[d],
            recv_sem=recv_sem.at[d], device_id=(pg, pc * 2 + parity), device_id_type=mesh_id)

    def go(d, c):
        to_owner(d).start()
        return c

    def done(d, c):
        to_owner(d).wait()
        return c

    lax.fori_loop(1, n, go, 0)
    inbox[column, g] = sums[column, g]
    lax.fori_loop(1, n, done, 0)
    total = jnp.zeros(mine_ref.shape, jnp.float32)
    for i in range(pairs):
        for j in range(groups):
            total = total + inbox[i, j]
    residual = (mine_ref[...] - total / rs_ref[...]) * on_ref[...]
    own_ref[...] = residual
    stage[...] = residual.astype(jnp.bfloat16)

    def to_all(d):
        pc, pg = peer(d)
        return pltpu.make_async_remote_copy(
            src_ref=stage, dst_ref=gathered.at[column, parity, g], send_sem=out_send.at[d],
            recv_sem=out_recv.at[d], device_id=(pg, pc * 2 + parity), device_id_type=mesh_id)

    def go_all(d, c):
        to_all(d).start()
        return c

    def done_all(d, c):
        to_all(d).wait()
        return c

    lax.fori_loop(1, n, go_all, 0)
    gathered[column, parity, g] = stage[...]
    lax.fori_loop(1, n, done_all, 0)
    share = pltpu.make_async_remote_copy(
        src_ref=gathered.at[:, parity], dst_ref=gathered.at[:, parity], send_sem=back_send,
        recv_sem=back_recv, device_id=partner, device_id_type=mesh_id)
    share.start()
    share.wait()
    for i in range(pairs):
        full_ref[i] = gathered[i].astype(jnp.float32)


def exchange(partial, mine, on, rs, groups, patches):
    lines = mine.shape[0]
    pairs = patches // 2
    shape = (pairs, 2, groups, lines, LANES)
    n = pairs * groups
    dma = pltpu.SemaphoreType.DMA
    vmem = pl.BlockSpec(memory_space=pltpu.VMEM)
    full, own = pl.pallas_call(
        exchange_kernel,
        in_specs=[vmem] * 4,
        out_specs=[vmem] * 2,
        out_shape=[jax.ShapeDtypeStruct(shape, jnp.float32),
                   jax.ShapeDtypeStruct((lines, LANES), jnp.float32)],
        scratch_shapes=[pltpu.VMEM((pairs, groups, lines, LANES), jnp.float32),
                        pltpu.VMEM((pairs, groups, lines, LANES), jnp.float32),
                        pltpu.VMEM((pairs, groups, lines, LANES), jnp.float32),
                        pltpu.VMEM((lines, LANES), jnp.bfloat16),
                        pltpu.VMEM(shape, jnp.bfloat16),
                        dma((n,)), dma((n,)), dma, dma, dma((n,)), dma((n,)), dma, dma],
        compiler_params=pltpu.CompilerParams(collective_id=0, has_side_effects=True),
        name="exchange",
    )(partial.reshape(shape), mine, on, rs)
    return full.reshape(partial.shape), own


def smem():
    return pl.BlockSpec(memory_space=pltpu.SMEM)


def forward(volume, lo, frac, win, base, first):
    blocks, slices, _ = volume.shape
    nb = 8
    lines = ANG_SUB * RAYS // 16
    return pl.pallas_call(
        lambda *refs: forward_kernel(nb, *refs),
        grid=(blocks // nb,),
        in_specs=[smem(), smem(), smem(), smem(),
                  pl.BlockSpec((nb, slices, VOX), lambda i: (i, 0, 0)),
                  pl.BlockSpec((ANG_SUB, VOX), lambda i: (0, 0))],
        out_specs=[pl.BlockSpec((lines, LANES), lambda i: (0, 0)),
                   pl.BlockSpec((nb, ANG_SUB * R, VOX), lambda i: (i, 0, 0))],
        out_shape=[jax.ShapeDtypeStruct((lines, LANES), jnp.float32),
                   jax.ShapeDtypeStruct((blocks, ANG_SUB * R, VOX), jnp.bfloat16)],
        scratch_shapes=[pltpu.VMEM((ANG_SUB * R, VOX), jnp.float32),
                        pltpu.VMEM((LANES, VOX), jnp.bfloat16),
                        pltpu.VMEM((ANG_SUB * TALL, LANES), jnp.float32)],
        compiler_params=pltpu.CompilerParams(vmem_limit_bytes=VMEM_LIMIT),
        name="forward",
    )(lo, frac, win, first, volume, base)


def backward(volume, residual, lo, win, foot, first):
    blocks, slices, _ = volume.shape
    nb = 8
    return pl.pallas_call(
        lambda *refs: backward_kernel(nb, *refs),
        grid=(blocks // nb,),
        in_specs=[smem(), smem(), smem(),
                  pl.BlockSpec((nb, slices, VOX), lambda i: (i, 0, 0)),
                  pl.BlockSpec((nb, ANG_SUB * R, VOX), lambda i: (i, 0, 0)),
                  pl.BlockSpec(residual.shape, lambda i: (0, 0))],
        out_specs=pl.BlockSpec((nb, slices, VOX), lambda i: (i, 0, 0)),
        out_shape=jax.ShapeDtypeStruct(volume.shape, jnp.float32),
        scratch_shapes=[pltpu.VMEM((TALL, LANES), jnp.float32),
                        pltpu.VMEM((ANG_SUB * RAYS, LANES), jnp.float32)],
        compiler_params=pltpu.CompilerParams(vmem_limit_bytes=VMEM_LIMIT),
        name="backward",
    )(lo, win, first, volume, foot, residual)


def own_ray_sums(first_row, rows):
    count = rows * RAYS_TILE
    padded = -(-count // 1024) * 1024
    idx = jnp.minimum(jnp.arange(padded, dtype=jnp.int32), count - 1)
    row = first_row + idx // RAYS_TILE
    ray = ((row % NTILE) * RAYS_TILE + idx % RAYS_TILE).astype(jnp.float32) + (0.5 - RAYS * 0.5)
    angle = row // NTILE
    big, small = [], []
    for subset in range(SUBSETS):
        th = angles(subset)
        pairs = [sorted((math.cos(t), math.sin(t)), key=abs) for t in th]
        sign = jnp.zeros((padded,), jnp.float32)
        b, s = sign, sign
        for a in range(ANG_SUB):
            b = jnp.where(angle == a, np.float32(pairs[a][1]), b)
            s = jnp.where(angle == a, np.float32(pairs[a][0]), s)
        big.append(b)
        small.append(s)
    shape = (SUBSETS, padded // LANES, LANES)
    big = jnp.stack(big).reshape(shape)
    small = jnp.stack(small).reshape(shape)
    rays = jnp.broadcast_to(ray.reshape(1, padded // LANES, LANES), shape)
    sums = pl.pallas_call(
        ray_sum_kernel,
        out_shape=jax.ShapeDtypeStruct(shape, jnp.float32),
        name="raysum",
    )(big, small, rays)
    return sums.reshape(SUBSETS, padded)[:, :count]


def placing(place, subset):
    half = IMG_BLK * BLK_SIDE * 0.5
    x = (place % IMG_BLK).astype(jnp.float32) * BLK_SIDE + (BLK_SIDE * 0.5 - half)
    y = (place // IMG_BLK).astype(jnp.float32) * BLK_SIDE + (BLK_SIDE * 0.5 - half)
    cosine = np.cos(np.array(angles(subset))).astype(np.float32)
    sine = np.sin(np.array(angles(subset))).astype(np.float32)
    z = x[:, None] * cosine + y[:, None] * sine + (RAYS * 0.5 - 0.5)
    low = jnp.floor(z)
    lo = low.astype(jnp.int32)
    tile = jnp.arange(TALL // SPAN, dtype=jnp.int32)
    touched = jnp.any(((lo - PAD) // SPAN)[:, :, None] == tile, axis=0)
    touched |= jnp.any(((lo + R + PAD) // SPAN)[:, :, None] == tile, axis=0)
    cleared = touched | jnp.pad(touched[:, :-1], ((0, 0), (1, 0)))
    win = jnp.stack([touched.reshape(-1), cleared.reshape(-1)]).astype(jnp.int32)
    return lo, (z - low) * (1.0 / spread), win


def shards(volume, block_place, measured, live_rays):
    groups = lax.axis_size("group")
    patches = lax.axis_size("patch")
    group_index = lax.axis_index("group")
    patch_index = lax.axis_index("patch")
    slices = volume.shape[1]
    slab_rows = ANG_SUB * NTILE // patches
    rows = slab_rows // groups
    first_row = patch_index * slab_rows + group_index * rows
    lines = rows * RAYS_TILE * slices // LANES
    per = LANES // slices
    sums = own_ray_sums(first_row, rows)
    estimate = volume
    own_residual = None
    for subset in range(SUBSETS):
        base, first = geometry(subset)
        lo, frac, win = placing(block_place, subset)
        partial, foot = forward(estimate, lo, frac, win, base, first)
        mine = lax.dynamic_slice_in_dim(measured[subset], group_index * rows, rows, 0)
        live = lax.dynamic_slice_in_dim(live_rays[subset], first_row, rows, 0)
        on = jnp.arange(RAYS_TILE, dtype=jnp.int32)[None, :] < live[:, None]
        on = jnp.broadcast_to(on[:, :, None], (rows, RAYS_TILE, slices)).reshape(lines, LANES)
        rs = jnp.maximum(sums[subset], 1.0).reshape(lines, per, 1)
        rs = jnp.broadcast_to(rs, (lines, per, slices)).reshape(lines, LANES)
        full, own = exchange(partial, mine.reshape(lines, LANES), on.astype(jnp.float32), rs, groups, patches)
        own_residual = own.reshape(rows, RAYS_TILE * slices)
        estimate = backward(estimate, full, lo, win, foot, first)
    return (estimate, own_residual[None])


def solution(mesh):
    return jax.shard_map(
        shards,
        mesh=mesh,
        in_specs=(
            P(("group", "patch"), None, None),
            P(("group", "patch")),
            P(None, "patch", None),
            P(),
        ),
        out_specs=(P(("group", "patch"), None, None), P("group", "patch", None)),
        check_vma=False,
    )
```

```python
import math

import jax
import jax.numpy as jnp
import numpy as np
from jax import lax
from jax.experimental import pallas as pl
from jax.experimental.pallas import tpu as pltpu
from jax.sharding import PartitionSpec as P

IMG_BLK = 64
BLK_SIDE = 32
RAYS_TILE = 48
NTILE = 64
ANG_SUB = 8
SUBSETS = 2

spread = 1.5
relax = 0.9

SUB = 8
NQ = (BLK_SIDE // SUB) ** 2
R = 16
VOX = BLK_SIDE * BLK_SIDE
RAYS = NTILE * RAYS_TILE
LANES = 128
PAD = 32
SPAN = 128
TALL = RAYS + SPAN
VMEM_LIMIT = 60 * 1024 * 1024


def angles(subset):
    return [math.pi * (a * SUBSETS + subset) / (ANG_SUB * SUBSETS) for a in range(ANG_SUB)]


def geometry(subset):
    v = np.arange(VOX)
    col = (v % BLK_SIDE) + 0.5 - BLK_SIDE / 2
    row = (v // BLK_SIDE) + 0.5 - BLK_SIDE / 2
    q_of = (v // BLK_SIDE // SUB) * (BLK_SIDE // SUB) + (v % BLK_SIDE) // SUB
    base = np.zeros((ANG_SUB, VOX), np.float64)
    first = np.zeros((ANG_SUB, NQ), np.int64)
    for a, theta in enumerate(angles(subset)):
        off = col * math.cos(theta) + row * math.sin(theta)
        for q in range(NQ):
            mine = q_of == q
            first[a, q] = math.floor(off[mine].min() - spread)
            base[a, mine] = off[mine] - first[a, q]
    return base.astype(np.float32), first.astype(np.int32)


def fill_grid(base_ref, e_scr):
    ray = lax.broadcasted_iota(jnp.int32, (R, VOX), 0).astype(jnp.float32)
    for a in range(ANG_SUB):
        e_scr[a * R:(a + 1) * R, :] = (base_ref[a:a + 1, :] - ray) * (1.0 / spread)


def make_footprint(e_scr, f_scr, frac_ref, b):
    for a in range(ANG_SUB):
        t = e_scr[a * R:(a + 1) * R, :] + frac_ref[b, a]
        bump = jnp.maximum(1.0 - t * t, 0.0)
        f_scr[a * R:(a + 1) * R, :] = (bump * bump).astype(jnp.bfloat16)


TILES = RAYS // SPAN


def list_tiles(win_ref, tiles):
    def step(i, n):
        hit = win_ref[i]
        tiles[n] = i
        return n + hit

    n = lax.fori_loop(0, ANG_SUB * TILES, step, 0)
    tiles[n] = tiles[jnp.maximum(n - 1, 0)]
    return (n + 1) // 2


def over_tiles(tiles, half_count, body):
    def pair(i, c):
        for j in range(2):
            at = tiles[2 * i + j]
            body(at // TILES, lax.rem(at, TILES))
        return c

    lax.fori_loop(0, half_count, pair, 0)


def aligned(x, m):
    return pl.multiple_of(x, m)


def forward_kernel(nb, lo_ref, frac_ref, win_ref, first_ref, vol_ref, base_ref, out_ref,
                   e_scr, f_even, f_odd, m_scr, acc, tiles):
    f_bufs = (f_even, f_odd)
    step = pl.program_id(0)

    @pl.when(step == 0)
    def _():
        fill_grid(base_ref, e_scr)
        v = lax.broadcasted_iota(jnp.int32, (LANES, VOX), 1)
        line = lax.broadcasted_iota(jnp.int32, (LANES, VOX), 0)
        q_of = (v // (BLK_SIDE * SUB)) * (BLK_SIDE // SUB) + (v % BLK_SIDE) // SUB
        m_scr[...] = jnp.where(q_of == line // 8, 1.0, 0.0).astype(jnp.bfloat16)
        zero = jnp.zeros((2 * SPAN, LANES), jnp.float32)

        tiles[ANG_SUB * TILES + 1] = list_tiles(win_ref, tiles)

        def clear(a, i):
            acc[pl.ds(aligned(a * TALL + i * SPAN, SPAN), 2 * SPAN), :] = zero

        over_tiles(tiles, tiles[ANG_SUB * TILES + 1], clear)

    for i in range(nb):
        b = step * nb + i
        f_scr = f_bufs[i % 2]
        make_footprint(e_scr, f_scr, frac_ref, b)
        rounded = vol_ref[i].astype(jnp.bfloat16)
        spreadv = jnp.tile(rounded, (NQ, 1)) * m_scr[...]
        part = lax.dot_general(f_scr[...], spreadv, (((1,), (1,)), ((), ())),
                               preferred_element_type=jnp.float32)
        for a in range(ANG_SUB):
            at = pl.ds(a * TALL + PAD + lo_ref[b, a], R)
            acc[at, :] += part[a * R:(a + 1) * R, :]

    @pl.when(step == pl.num_programs(0) - 1)
    def _():
        out_ref[...] = jnp.zeros_like(out_ref)
        span = SPAN
        lane_q = lax.broadcasted_iota(jnp.int32, (span, LANES), 1) // 8
        row_j = lax.broadcasted_iota(jnp.int32, (span, LANES), 0) % 16
        pick = lane_q == row_j

        def merge(a, i):
            k = i * span
            total = jnp.zeros((span, LANES), jnp.float32)
            for q in range(NQ):
                src = a * TALL + PAD + k - first_ref[a, q]
                total = jnp.where(lane_q == q, acc[pl.ds(src, span), :], total)
            for s in (64, 32, 16, 8):
                total = total + pltpu.roll(total, s, 1)
            total = jnp.where(pick, total, 0.0)
            out = jnp.sum(total.reshape(span // 16, 16, LANES), axis=1)
            out_ref[pl.ds(aligned(a * (RAYS // 16) + i * 8, 8), 8), :] = out

        over_tiles(tiles, tiles[ANG_SUB * TILES + 1], merge)


def backward_kernel(nb, lo_ref, frac_ref, win_ref, first_ref, vol_ref, base_ref, res_ref, out_ref,
                    e_scr, f_even, f_odd, rb, dd, tiles):
    f_bufs = (f_even, f_odd)
    step = pl.program_id(0)

    @pl.when(step == 0)
    def _():
        fill_grid(base_ref, e_scr)
        span = SPAN
        lane_q = lax.broadcasted_iota(jnp.int32, (span, LANES), 1) // 8
        row_j = lax.broadcasted_iota(jnp.int32, (span, LANES), 0) % 16
        pick = lane_q == row_j
        fold = jnp.where(
            lax.broadcasted_iota(jnp.int32, (LANES, LANES), 0) % 8
            == lax.broadcasted_iota(jnp.int32, (LANES, LANES), 1) % 8, 1.0, 0.0).astype(jnp.bfloat16)

        count = list_tiles(win_ref, tiles)

        def widen(a, i):
            rows = res_ref[pl.ds(aligned(a * (RAYS // 16) + i * 8, 8), 8), :]
            wide = jnp.broadcast_to(rows[:, None, :], (8, 16, LANES)).reshape(span, LANES)
            wide = jnp.where(pick, wide, 0.0).astype(jnp.bfloat16)
            rb[pl.ds(aligned(a * TALL + PAD + i * span, 8), span), :] = jnp.dot(
                wide, fold, preferred_element_type=jnp.float32)

        def shift(a, i):
            k = i * span
            total = jnp.zeros((span, LANES), jnp.float32)
            for q in range(NQ):
                src = a * TALL + PAD + k + first_ref[a, q]
                total = jnp.where(lane_q == q, rb[pl.ds(src, span), :], total)
            dd[pl.ds(aligned(a * RAYS + k, span), span), :] = total

        over_tiles(tiles, count, widen)
        over_tiles(tiles, count, shift)

    width = SUB * BLK_SIDE
    group = BLK_SIDE // SUB
    lane = lax.broadcasted_iota(jnp.int32, (8, width), 1)
    col_group = (lane % BLK_SIDE) // SUB

    for i in range(nb):
        b = step * nb + i
        f_scr = f_bufs[i % 2]
        make_footprint(e_scr, f_scr, frac_ref, b)
        rows = jnp.concatenate(
            [dd[pl.ds(a * RAYS + lo_ref[b, a], R), :] for a in range(ANG_SUB)], axis=0)
        turned = jnp.transpose(rows)
        ones = jnp.ones((8, ANG_SUB * R), jnp.float32)
        for g in range(group):
            lhs = jnp.concatenate([turned[g * 32:(g + 1) * 32], ones], axis=0).astype(jnp.bfloat16)
            at = slice(g * width, (g + 1) * width)
            part = jnp.dot(lhs, f_scr[:, at], preferred_element_type=jnp.float32)
            back = part[0:8]
            for j in range(1, group):
                back = jnp.where(col_group == j, part[j * 8:(j + 1) * 8], back)
            col_sum = part[32:40]
            out_ref[i, :, at] = jnp.maximum(vol_ref[i, :, at] + relax * back / col_sum, 0.0)


def ray_sum_kernel(c_ref, s_ref, k_ref, out_ref):
    side = IMG_BLK * BLK_SIDE
    half = side * 0.5
    for u in range(c_ref.shape[0]):
        cs = c_ref[u] * (1.0 / spread)
        sn = s_ref[u] * (1.0 / spread)
        inv = 1.0 / cs
        ray = k_ref[u] * (1.0 / spread)

        def row(i, total):
            y = i.astype(jnp.float32) + (0.5 - half)
            w = ray - y * sn
            mid = jnp.clip(jnp.floor(w * inv) + 0.5, 2.5 - half, half - 2.5)
            t0 = mid * cs - w
            for t in (t0 - 2 * cs, t0 - cs, t0, t0 + cs, t0 + 2 * cs):
                bump = jnp.maximum(1.0 - t * t, 0.0)
                total = total + bump * bump
            return total

        out_ref[u] = lax.fori_loop(0, side, row, jnp.zeros(out_ref.shape[1:], jnp.float32), unroll=8)


def exchange_kernel(part_ref, mine_ref, on_ref, rs_ref, full_ref, own_ref,
                    half, inbox, sums, stage, gathered, send_sem, recv_sem,
                    pair_send, pair_recv, out_send, out_recv, back_send, back_recv):
    g, p = lax.axis_index("group"), lax.axis_index("patch")
    groups, pairs = inbox.shape[1], inbox.shape[0]
    n = groups * pairs
    parity, column = lax.rem(p, 2), p // 2
    me = column * groups + g
    partner = (g, column * 2 + 1 - parity)
    mesh_id = pl.DeviceIdType.MESH

    def peer(d):
        at = lax.rem(me + d, n)
        return at // groups, lax.rem(at, groups)

    barrier = pltpu.get_barrier_semaphore()
    pl.semaphore_signal(barrier, inc=1, device_id=partner, device_id_type=mesh_id)

    def greet(d, c):
        pc, pg = peer(d)
        pl.semaphore_signal(barrier, inc=1, device_id=(pg, pc * 2 + parity), device_id_type=mesh_id)
        return c

    lax.fori_loop(1, n, greet, 0)
    pl.semaphore_wait(barrier, n)

    swap = pltpu.make_async_remote_copy(
        src_ref=part_ref.at[:, 1 - parity], dst_ref=half, send_sem=pair_send, recv_sem=pair_recv,
        device_id=partner, device_id_type=mesh_id)
    swap.start()
    swap.wait()
    for i in range(pairs):
        sums[i] = part_ref[i, parity] + half[i]

    def to_owner(d):
        pc, pg = peer(d)
        return pltpu.make_async_remote_copy(
            src_ref=sums.at[pc, pg], dst_ref=inbox.at[column, g], send_sem=send_sem.at[d],
            recv_sem=recv_sem.at[d], device_id=(pg, pc * 2 + parity), device_id_type=mesh_id)

    def go(d, c):
        to_owner(d).start()
        return c

    def done(d, c):
        to_owner(d).wait()
        return c

    lax.fori_loop(1, n, go, 0)
    inbox[column, g] = sums[column, g]
    lax.fori_loop(1, n, done, 0)
    total = jnp.zeros(mine_ref.shape, jnp.float32)
    for i in range(pairs):
        for j in range(groups):
            total = total + inbox[i, j]
    residual = (mine_ref[...] - total / rs_ref[...]) * on_ref[...]
    own_ref[...] = residual
    stage[...] = residual.astype(jnp.bfloat16)

    def to_all(d):
        pc, pg = peer(d)
        return pltpu.make_async_remote_copy(
            src_ref=stage, dst_ref=gathered.at[column, parity, g], send_sem=out_send.at[d],
            recv_sem=out_recv.at[d], device_id=(pg, pc * 2 + parity), device_id_type=mesh_id)

    def go_all(d, c):
        to_all(d).start()
        return c

    def done_all(d, c):
        to_all(d).wait()
        return c

    lax.fori_loop(1, n, go_all, 0)
    gathered[column, parity, g] = stage[...]
    lax.fori_loop(1, n, done_all, 0)
    share = pltpu.make_async_remote_copy(
        src_ref=gathered.at[:, parity], dst_ref=gathered.at[:, parity], send_sem=back_send,
        recv_sem=back_recv, device_id=partner, device_id_type=mesh_id)
    share.start()
    share.wait()
    for i in range(pairs):
        full_ref[i] = gathered[i].astype(jnp.float32)


def exchange(partial, mine, on, rs, groups, patches):
    lines = mine.shape[0]
    pairs = patches // 2
    shape = (pairs, 2, groups, lines, LANES)
    n = pairs * groups
    dma = pltpu.SemaphoreType.DMA
    vmem = pl.BlockSpec(memory_space=pltpu.VMEM)
    full, own = pl.pallas_call(
        exchange_kernel,
        in_specs=[vmem] * 4,
        out_specs=[vmem] * 2,
        out_shape=[jax.ShapeDtypeStruct(shape, jnp.float32),
                   jax.ShapeDtypeStruct((lines, LANES), jnp.float32)],
        scratch_shapes=[pltpu.VMEM((pairs, groups, lines, LANES), jnp.float32),
                        pltpu.VMEM((pairs, groups, lines, LANES), jnp.float32),
                        pltpu.VMEM((pairs, groups, lines, LANES), jnp.float32),
                        pltpu.VMEM((lines, LANES), jnp.bfloat16),
                        pltpu.VMEM(shape, jnp.bfloat16),
                        dma((n,)), dma((n,)), dma, dma, dma((n,)), dma((n,)), dma, dma],
        compiler_params=pltpu.CompilerParams(collective_id=0, has_side_effects=True),
        name="exchange",
    )(partial.reshape(shape), mine, on, rs)
    return full.reshape(partial.shape), own


def smem():
    return pl.BlockSpec(memory_space=pltpu.SMEM)


def forward(volume, lo, frac, win, base, first):
    blocks, slices, _ = volume.shape
    nb = 8
    lines = ANG_SUB * RAYS // 16
    return pl.pallas_call(
        lambda *refs: forward_kernel(nb, *refs),
        grid=(blocks // nb,),
        in_specs=[smem(), smem(), smem(), smem(),
                  pl.BlockSpec((nb, slices, VOX), lambda i: (i, 0, 0)),
                  pl.BlockSpec((ANG_SUB, VOX), lambda i: (0, 0))],
        out_specs=pl.BlockSpec((lines, LANES), lambda i: (0, 0)),
        out_shape=jax.ShapeDtypeStruct((lines, LANES), jnp.float32),
        scratch_shapes=[pltpu.VMEM((ANG_SUB * R, VOX), jnp.float32),
                        pltpu.VMEM((ANG_SUB * R, VOX), jnp.bfloat16),
                        pltpu.VMEM((ANG_SUB * R, VOX), jnp.bfloat16),
                        pltpu.VMEM((LANES, VOX), jnp.bfloat16),
                        pltpu.VMEM((ANG_SUB * TALL, LANES), jnp.float32),
                        pltpu.SMEM((ANG_SUB * TILES + 2,), jnp.int32)],
        compiler_params=pltpu.CompilerParams(vmem_limit_bytes=VMEM_LIMIT),
        name="forward",
    )(lo, frac, win, first, volume, base)


def backward(volume, residual, lo, frac, win, base, first):
    blocks, slices, _ = volume.shape
    nb = 8
    return pl.pallas_call(
        lambda *refs: backward_kernel(nb, *refs),
        grid=(blocks // nb,),
        in_specs=[smem(), smem(), smem(), smem(),
                  pl.BlockSpec((nb, slices, VOX), lambda i: (i, 0, 0)),
                  pl.BlockSpec((ANG_SUB, VOX), lambda i: (0, 0)),
                  pl.BlockSpec(residual.shape, lambda i: (0, 0))],
        out_specs=pl.BlockSpec((nb, slices, VOX), lambda i: (i, 0, 0)),
        out_shape=jax.ShapeDtypeStruct(volume.shape, jnp.float32),
        scratch_shapes=[pltpu.VMEM((ANG_SUB * R, VOX), jnp.float32),
                        pltpu.VMEM((ANG_SUB * R, VOX), jnp.bfloat16),
                        pltpu.VMEM((ANG_SUB * R, VOX), jnp.bfloat16),
                        pltpu.VMEM((ANG_SUB * TALL, LANES), jnp.float32),
                        pltpu.VMEM((ANG_SUB * RAYS, LANES), jnp.float32),
                        pltpu.SMEM((ANG_SUB * TILES + 2,), jnp.int32)],
        compiler_params=pltpu.CompilerParams(vmem_limit_bytes=VMEM_LIMIT),
        name="backward",
    )(lo, frac, win, first, volume, base, residual)


def own_ray_sums(first_row, rows):
    count = rows * RAYS_TILE
    padded = -(-count // 1024) * 1024
    idx = jnp.minimum(jnp.arange(padded, dtype=jnp.int32), count - 1)
    row = first_row + idx // RAYS_TILE
    ray = ((row % NTILE) * RAYS_TILE + idx % RAYS_TILE).astype(jnp.float32) + (0.5 - RAYS * 0.5)
    angle = row // NTILE
    big, small = [], []
    for subset in range(SUBSETS):
        th = angles(subset)
        pairs = [sorted((math.cos(t), math.sin(t)), key=abs) for t in th]
        sign = jnp.zeros((padded,), jnp.float32)
        b, s = sign, sign
        for a in range(ANG_SUB):
            b = jnp.where(angle == a, np.float32(pairs[a][1]), b)
            s = jnp.where(angle == a, np.float32(pairs[a][0]), s)
        big.append(b)
        small.append(s)
    shape = (SUBSETS, padded // LANES, LANES)
    big = jnp.stack(big).reshape(shape)
    small = jnp.stack(small).reshape(shape)
    rays = jnp.broadcast_to(ray.reshape(1, padded // LANES, LANES), shape)
    sums = pl.pallas_call(
        ray_sum_kernel,
        out_shape=jax.ShapeDtypeStruct(shape, jnp.float32),
        name="raysum",
    )(big, small, rays)
    return sums.reshape(SUBSETS, padded)[:, :count]


def placing(place, subset):
    half = IMG_BLK * BLK_SIDE * 0.5
    x = (place % IMG_BLK).astype(jnp.float32) * BLK_SIDE + (BLK_SIDE * 0.5 - half)
    y = (place // IMG_BLK).astype(jnp.float32) * BLK_SIDE + (BLK_SIDE * 0.5 - half)
    cosine = np.cos(np.array(angles(subset))).astype(np.float32)
    sine = np.sin(np.array(angles(subset))).astype(np.float32)
    z = x[:, None] * cosine + y[:, None] * sine + (RAYS * 0.5 - 0.5)
    low = jnp.floor(z)
    lo = low.astype(jnp.int32)
    tile = jnp.arange(TILES, dtype=jnp.int32)
    touched = jnp.any(((lo - PAD) // SPAN)[:, :, None] == tile, axis=0)
    touched |= jnp.any(((lo + R + PAD) // SPAN)[:, :, None] == tile, axis=0)
    win = touched.reshape(-1).astype(jnp.int32)
    return lo, (z - low) * (1.0 / spread), win


def shards(volume, block_place, measured, live_rays):
    groups = lax.axis_size("group")
    patches = lax.axis_size("patch")
    group_index = lax.axis_index("group")
    patch_index = lax.axis_index("patch")
    slices = volume.shape[1]
    slab_rows = ANG_SUB * NTILE // patches
    rows = slab_rows // groups
    first_row = patch_index * slab_rows + group_index * rows
    lines = rows * RAYS_TILE * slices // LANES
    per = LANES // slices
    sums = own_ray_sums(first_row, rows)
    estimate = volume
    own_residual = None
    for subset in range(SUBSETS):
        base, first = geometry(subset)
        lo, frac, win = placing(block_place, subset)
        partial = forward(estimate, lo, frac, win, base, first)
        mine = lax.dynamic_slice_in_dim(measured[subset], group_index * rows, rows, 0)
        live = lax.dynamic_slice_in_dim(live_rays[subset], first_row, rows, 0)
        on = jnp.arange(RAYS_TILE, dtype=jnp.int32)[None, :] < live[:, None]
        on = jnp.broadcast_to(on[:, :, None], (rows, RAYS_TILE, slices)).reshape(lines, LANES)
        rs = jnp.maximum(sums[subset], 1.0).reshape(lines, per, 1)
        rs = jnp.broadcast_to(rs, (lines, per, slices)).reshape(lines, LANES)
        full, own = exchange(partial, mine.reshape(lines, LANES), on.astype(jnp.float32), rs, groups, patches)
        own_residual = own.reshape(rows, RAYS_TILE * slices)
        estimate = backward(estimate, full, lo, frac, win, base, first)
    return (estimate, own_residual[None])


def solution(mesh):
    return jax.shard_map(
        shards,
        mesh=mesh,
        in_specs=(
            P(("group", "patch"), None, None),
            P(("group", "patch")),
            P(None, "patch", None),
            P(),
        ),
        out_specs=(P(("group", "patch"), None, None), P("group", "patch", None)),
        check_vma=False,
    )
```
